32 devices in a mesh: span: 8 (over z, y), plane: 4 (over x, core).
Axes of the slice: x: 2, y: 2, z: 4, core: 2. Of those that a mesh axis runs over, the one named last changes fastest.
Arguments:
- adjoint: float32 [3, 32, 81, 512], P(None, 'span', None, 'plane'), may hold values from -6 to 6
- checkpoints: bfloat16 [8, 2, 32, 81, 512], P(None, None, 'span', None, 'plane'), may hold values from -4 to 4
- checkpoint_step: int32 [3], replicated, may hold values from 0 to 7
- metric: float32 [2, 512], P(None, 'plane'), may hold values from 0.004 to 0.016
- helmholtz_inverse: float32 [32, 81, 81], P('span'), may hold values from -0.08 to 0.8
- wall_element: int32 [1024, 2], replicated, may hold values from 0 to 511
- wall_local: int32 [1024, 2], replicated, may hold values from 0 to 80
- wall_weight: float32 [32, 1024], P('span'), may hold values from 0.7 to 140
Outputs:
- adjoint_next: float32 [3, 32, 81, 512], P(None, 'span', None, 'plane')
- control_gradient: float32 [32, 1024], P('span', 'plane')
The draws below stay inside these ranges and needn't reach their ends.
All inputs are finite; a program needn't handle non-finite values.
Results may differ from the reference program's by a relative error of at most 0.00065.
Values may be sent and summed in bfloat16 or wider, within the bound.
A program may use at most 128 MiB of HBM per device.

```python
import math
import jax
import jax.numpy as jnp
import numpy as np
from jax import lax

P_SIZE = 8
Q = 81
NZ = 32
NEL = 512
NWALL = 1024
NCK = 8
NSTEP = 3


def draw_helmholtz_inverse(key, part):
    key_diag = jax.random.fold_in(key, 11)
    key_off = jax.random.fold_in(key, 12)
    diagonal = jnp.exp(jax.random.uniform(key_diag, (NZ, Q), jnp.float32, math.log(0.3), math.log(0.8)))
    spread = jnp.clip(0.02 * jax.random.normal(key_off, (NZ, Q, Q), jnp.float32), -0.08, 0.08)
    unit_matrix = jnp.eye(Q, dtype=jnp.float32)
    return diagonal[:, :, None] * unit_matrix + spread * (1.0 - unit_matrix)


def draw_wall_weight(key, part):
    row_pos = jnp.arange(NZ, dtype=jnp.float32)[:, None] / (NZ - 1)
    col_pos = jnp.arange(NWALL, dtype=jnp.float32)[None, :] / (NWALL - 1)
    exponent = 0.5
    factor = jnp.exp(jax.random.uniform(jax.random.fold_in(key, 21), (NZ, NWALL), jnp.float32, math.log(0.7), math.log(1.4)))
    return factor * jnp.power(10.0, exponent * (row_pos + col_pos))


def touch_ends(drawn, stream_key, smallest, top_value):
    place = [jax.random.randint(jax.random.fold_in(stream_key, axis), (), 0, length) for axis, length in enumerate(drawn.shape)]
    main_axis = drawn.shape.index(max(drawn.shape))
    next_to = place[:main_axis] + [(place[main_axis] + 1) % drawn.shape[main_axis]] + place[main_axis + 1:]
    return drawn.at[tuple(place)].set(smallest).at[tuple(next_to)].set(top_value)


def shard_levels(rng, shape, shards, smallest, top_value):
    loudness = 1.0
    for dim, blocks in shards:
        draws = jax.random.uniform(jax.random.fold_in(jax.random.fold_in(rng, 6), dim), (blocks,), jnp.float32, smallest / len(shards), top_value / len(shards))
        loudness = loudness * jnp.repeat(jnp.exp(draws), shape[dim] // blocks).reshape((-1,) + (1,) * (len(shape) - 1 - dim))
    return loudness


def normal_values(stream_key, shape, scale, reach, split=(), kind=jnp.bfloat16):
    entries = scale * jax.random.normal(stream_key, shape, jnp.float32)
    if split:
        entries = entries * shard_levels(stream_key, shape, split, -0.22, 0.18)
    return jnp.clip(entries, -reach, reach).astype(kind)


def setup_inputs(seed: int = 0) -> dict:
    keys = jax.random.split(jax.random.key(seed), 9)
    adjoint = normal_values(keys[0], (3, NZ, Q, NEL), 1.0, 6.0, ((1, 8), (3, 4)), jnp.float32)
    checkpoints = normal_values(keys[1], (NCK, 2, NZ, Q, NEL), 0.7, 4.0, ((2, 8), (4, 4)))
    checkpoint_step = jax.random.randint(keys[2], (NSTEP,), 0, NCK).astype(jnp.int32)
    metric = jnp.clip(jnp.exp(math.log(0.016) - 1.3862944 * jax.random.uniform(keys[3], (2, NEL), jnp.float32) ** shard_levels(keys[3], (2, NEL), ((1, 4),), -0.2, 0.2)), 0.004, 0.016)
    helmholtz_inverse = draw_helmholtz_inverse(jax.random.fold_in(keys[8], 71), 0)
    wall_element = touch_ends(jax.random.randint(keys[5], (NWALL, 2), 0, NEL), jax.random.fold_in(keys[5], 1), 0, NEL - 1).astype(jnp.int32)
    wall_local = touch_ends(jax.random.randint(keys[6], (NWALL, 2), 0, Q), jax.random.fold_in(keys[6], 1), 0, Q - 1).astype(jnp.int32)
    wall_weight = draw_wall_weight(jax.random.fold_in(keys[8], 71), 0)
    return {"adjoint": adjoint, "checkpoints": checkpoints, "checkpoint_step": checkpoint_step, "metric": metric, "helmholtz_inverse": helmholtz_inverse, "wall_element": wall_element, "wall_local": wall_local, "wall_weight": wall_weight}


HIGHEST = lax.Precision.HIGHEST

def chebyshev_matrix(degree):
    points = np.arange(degree + 1)
    abscissa = np.cos(np.pi * points / degree)
    signed = np.where((points == 0) | (points == degree), 2.0, 1.0) * (-1.0) ** points
    spacing = abscissa[:, None] - abscissa[None, :] + np.eye(degree + 1)
    matrix = signed[:, None] / signed[None, :] / spacing
    return matrix - np.eye(degree + 1) * np.sum(matrix, axis=1)[:, None]

def fourier_table(length):
    row_index = np.arange(length)[:, None]
    column = np.arange(length)[None, :]
    wavenumber = (row_index + 1) // 2
    phase_angle = 2.0 * np.pi * wavenumber * column / length
    parity = row_index % 2
    base_rows = np.where(row_index == 0, 1.0, np.where(parity == 1, np.cos(phase_angle), np.sin(phase_angle)))
    row_scale = np.where((row_index == 0) | (row_index == length - 1), 1.0 / np.sqrt(length), np.sqrt(2.0 / length))
    return base_rows * row_scale

def transport(field_data, velocity, metric):
    side_nodes = P_SIZE + 1
    matrix = jnp.asarray(chebyshev_matrix(P_SIZE), jnp.float32)
    shaped = field_data.reshape(field_data.shape[0], field_data.shape[1], side_nodes, side_nodes, field_data.shape[3])
    first_dir = jnp.einsum('ai,czibe->czabe', matrix, shaped, precision=HIGHEST).reshape(field_data.shape)
    second_dir = jnp.einsum('bi,czaie->czabe', matrix, shaped, precision=HIGHEST).reshape(field_data.shape)
    speed_data = velocity.astype(jnp.float32)
    return field_data + speed_data[0] * (metric[0] * first_dir) + speed_data[1] * (metric[1] * second_dir)

def one_component(component, velocity, metric, helmholtz_inverse):
    advected = transport(component[None], velocity, metric)[0]
    basis_table = jnp.asarray(fourier_table(NZ), jnp.float32)
    coefficients = jnp.einsum('jz,zqe->jqe', basis_table, advected, precision=HIGHEST)
    solved = jnp.einsum('jqr,jre->jqe', helmholtz_inverse, coefficients, precision=HIGHEST)
    return jnp.einsum('jz,jqe->zqe', basis_table, solved, precision=HIGHEST)

def reference(adjoint, checkpoints, checkpoint_step, metric, helmholtz_inverse, wall_element, wall_local, wall_weight):
    gradient_sum = jnp.zeros((NZ, NWALL), jnp.float32)
    for substep in range(NSTEP):
        slot_index = checkpoint_step[substep]
        velocity = lax.dynamic_index_in_dim(checkpoints, slot_index, 0, keepdims=False)
        adjoint = lax.map(lambda component: one_component(component, velocity, metric, helmholtz_inverse), adjoint)
        values = adjoint[1][:, wall_local, wall_element]
        speeds = velocity[1][:, wall_local, wall_element].astype(jnp.float32)
        gradient_sum = gradient_sum + lax.optimization_barrier(jnp.sum(values * speeds, axis=2))
    weighted = wall_weight * gradient_sum
    inverse_rms = lax.rsqrt(jnp.mean(weighted * weighted) + 1e-06)
    return (adjoint, weighted * inverse_rms)
```

```python
import functools

import jax
import jax.numpy as jnp
import ml_dtypes
import numpy as np
from jax import lax
from jax.experimental import pallas as pl
from jax.experimental.pallas import tpu as pltpu
from jax.sharding import PartitionSpec as P

P_SIZE = 8
NSTEP = 3


HIGHEST = lax.Precision.HIGHEST


def chebyshev_matrix(degree):
    points = np.arange(degree + 1)
    abscissa = np.cos(np.pi * points / degree)
    signed = np.where((points == 0) | (points == degree), 2.0, 1.0) * (-1.0) ** points
    spacing = abscissa[:, None] - abscissa[None, :] + np.eye(degree + 1)
    matrix = signed[:, None] / signed[None, :] / spacing
    return matrix - np.eye(degree + 1) * np.sum(matrix, axis=1)[:, None]


def fourier_table(length):
    row_index = np.arange(length)[:, None]
    column = np.arange(length)[None, :]
    wavenumber = (row_index + 1) // 2
    phase_angle = 2.0 * np.pi * wavenumber * column / length
    parity = row_index % 2
    base_rows = np.where(
        row_index == 0, 1.0, np.where(parity == 1, np.cos(phase_angle), np.sin(phase_angle))
    )
    row_scale = np.where(
        (row_index == 0) | (row_index == length - 1), 1.0 / np.sqrt(length), np.sqrt(2.0 / length)
    )
    return base_rows * row_scale


def transport(field_data, velocity, metric):
    side_nodes = P_SIZE + 1
    matrix = jnp.asarray(chebyshev_matrix(P_SIZE), jnp.float32)
    shaped = field_data.reshape(
        field_data.shape[0], field_data.shape[1], side_nodes, side_nodes, field_data.shape[3]
    )
    first_dir = jnp.einsum("ai,czibe->czabe", matrix, shaped, precision=HIGHEST).reshape(
        field_data.shape
    )
    second_dir = jnp.einsum("bi,czaie->czabe", matrix, shaped, precision=HIGHEST).reshape(
        field_data.shape
    )
    speed_data = velocity.astype(jnp.float32)
    return (
        field_data
        + speed_data[0] * (metric[0] * first_dir)
        + speed_data[1] * (metric[1] * second_dir)
    )


def forward_modes(gathered):
    basis_table = jnp.asarray(fourier_table(gathered.shape[1]), jnp.float32)
    return jnp.einsum("jz,czqe->cjqe", basis_table, gathered, precision=HIGHEST)


def backward_planes(solved):
    basis_table = jnp.asarray(fourier_table(solved.shape[1]), jnp.float32)
    return jnp.einsum("jz,cjqe->czqe", basis_table, solved, precision=HIGHEST)


def solve_modes(inverse_block, coefficients):
    return jnp.einsum("jqr,cjre->cjqe", inverse_block, coefficients, precision=HIGHEST)


def to_plane_layout(point_data):
    return lax.all_to_all(point_data, "span", split_axis=1, concat_axis=3, tiled=True)


def wall_terms(field_one, speed_one, flat_index, inside, wall_count):
    rows = field_one.shape[0]
    values = jnp.take(field_one.reshape(rows, -1), flat_index, axis=1)
    speeds = jnp.take(speed_one.reshape(rows, -1), flat_index, axis=1).astype(jnp.float32)
    product = jnp.where(inside, values * speeds, 0.0).reshape(rows, wall_count, 2)
    return jnp.sum(product, axis=2)


def on_device(
    adjoint,
    checkpoints,
    checkpoint_step,
    metric,
    helmholtz_inverse,
    wall_element,
    wall_local,
    wall_weight,
):
    planes_dev = adjoint.shape[1]
    elems_dev = adjoint.shape[3]
    wall_count = wall_element.shape[0]
    span_count = lax.axis_size("span")
    share = elems_dev // span_count
    all_modes = lax.all_gather(helmholtz_inverse, "span", axis=0, tiled=True)
    offset = lax.axis_index("plane") * elems_dev
    local_element = wall_element - offset
    inside = ((local_element >= 0) & (local_element < elems_dev)).reshape(-1)
    flat_index = (wall_local * elems_dev + jnp.clip(local_element, 0, elems_dev - 1)).reshape(-1)
    velocity = jnp.stack([
        lax.dynamic_index_in_dim(checkpoints, checkpoint_step[s], 0, keepdims=False)
        for s in range(NSTEP)
    ])
    velocity = lax.all_to_all(velocity, "span", split_axis=4, concat_axis=2, tiled=True)
    field = lax.all_to_all(adjoint, "span", split_axis=3, concat_axis=1, tiled=True)
    scale = lax.dynamic_slice_in_dim(metric, lax.axis_index("span") * share, share, 1)
    product = 0.0
    for substep in range(NSTEP):
        advected = transport(field, velocity[substep], scale)
        field = backward_planes(solve_modes(all_modes, forward_modes(advected)))
        product = product + field[1] * velocity[substep, 1].astype(jnp.float32)
    both = to_plane_layout(jnp.concatenate([field, product[None]], axis=0))
    gathered = jnp.take(both[3].reshape(planes_dev, -1), flat_index, axis=1)
    partial_sum = jnp.where(inside, gathered, 0.0).reshape(planes_dev, wall_count, 2).sum(axis=2)
    weighted = wall_weight * partial_sum
    grad_share = lax.psum_scatter(weighted, "plane", scatter_dimension=1, tiled=True)
    square_total = lax.psum(jnp.sum(grad_share * grad_share), ("span", "plane"))
    inverse_rms = lax.rsqrt(square_total / (planes_dev * span_count * wall_count) + 1e-06)
    return (both[:3], grad_share * inverse_rms)


MESH = pl.DeviceIdType.MESH
F32 = jnp.float32
BF16 = jnp.bfloat16
LANES = 128


def swap_blocks(parts, share):
    count = len(parts)
    width = count * share
    lane = lax.broadcasted_iota(jnp.int32, parts[0].shape, 1)
    k = count // 2
    while k:
        upper = (lane // (k * share)) % 2 == 1
        new = list(parts)
        for i in range(count):
            if (i // k) % 2 == 0:
                a, b = parts[i], parts[i + k]
                new[i] = jnp.where(upper, pltpu.roll(b, k * share, 1), a)
                new[i + k] = jnp.where(upper, b, pltpu.roll(a, width - k * share, 1))
        parts = new
        k //= 2
    return parts


def coded(x):
    top = jnp.maximum(jnp.max(jnp.abs(x), axis=0, keepdims=True), 1e-30)
    return jnp.round(x * (32767.0 / top)).astype(jnp.int32), top * (1.0 / 32767.0)


def remote(src, dst, sem_out, sem_in, target):
    return pltpu.make_async_remote_copy(
        src_ref=src, dst_ref=dst, send_sem=sem_out, recv_sem=sem_in,
        device_id=target, device_id_type=MESH,
    )


def mode_block(x, eye, q):
    diag = jnp.sum(jnp.where(eye, x, 0.0), axis=0, keepdims=True)
    off = jnp.where(eye, 0.0, x)
    row = lax.broadcasted_iota(jnp.int32, x.shape, 0)
    power = power_of(jnp.max(jnp.abs(off), axis=0, keepdims=True))
    power_d = power_of(jnp.abs(diag))
    unit = diag * (32767.0 * jnp.exp2(-power_d))
    high = jnp.round(unit)
    low = jnp.round((unit - high) * 32767.0)
    whole = jnp.round(off * (32767.0 * jnp.exp2(-power)))
    for i, extra in enumerate((power, power_d, high, low)):
        whole = jnp.where(row == q + i, extra, whole)
    return whole.astype(jnp.int32).astype(jnp.int16)


def power_of(top):
    return jnp.ceil(jnp.log2(jnp.maximum(top, 1e-30)))


def mode_matrix(block, eye, q):
    x = block.astype(jnp.int32).astype(F32)
    scale = jnp.exp2(x[q:q + 1]) * (1.0 / 32767.0)
    diag = (x[q + 2:q + 3] + x[q + 3:q + 4] * (1.0 / 32767.0)) * (jnp.exp2(x[q + 1:q + 2]) * (1.0 / 32767.0))
    row = lax.broadcasted_iota(jnp.int32, x.shape, 0)
    return jnp.where(eye, diag, jnp.where(row < q, x, 0.0) * scale)


def step_kernel(spans, planes, zdev, q, qp,
                step_h, adj_h, ck_h, inv_h, metric_h, elem_h, local_h, weight_h, basis_h, diff_h, place_h,
                back, tback, weighted_ref, srcv,
                step_ref, adj_ref, ck_ref, inv_ref, metric_ref, elem_ref, local_ref, weight_ref,
                basis_ref, diff_ref, place_ref,
                home, vhome, vf, xs_ref, vs_ref, v0_ref, padded, inv16, modes_ref, tail,
                snd, tsnd, rcv, trc, vsnd, vrcv, wsnd, wrc,
                coef, solved, product, kept, modes_cat, bsnd, tbsnd,
                picks, keeps, wall, rows_in, part, wrcv, square, sems, sqsems, load_sem, local_sem):
    share = LANES // spans
    me, p = lax.axis_index("span"), lax.axis_index("plane")
    bulk = q - 1
    half = bulk // 2
    slabs = 3 * zdev
    wide = zdev * LANES

    barrier = pltpu.get_barrier_semaphore()
    for a in range(planes):
        for o in range(spans):
            if a or o:
                pl.semaphore_signal(
                    barrier, 1, device_id={"plane": (p + a) % planes, "span": (me + o) % spans},
                    device_id_type=MESH)
    names = ("inv", "step", "metric", "adj", "ck", "diff", "elem", "local", "place", "basis", "weight")
    pairs = ((inv_h, inv_ref), (step_h, step_ref), (metric_h, metric_ref), (adj_h, adj_ref), (ck_h, ck_ref),
             (diff_h, diff_ref), (elem_h, elem_ref), (local_h, local_ref), (place_h, place_ref),
             (basis_h, basis_ref), (weight_h, weight_ref))
    loads = {}
    for i, (src, dst) in enumerate(pairs):
        loads[names[i]] = pltpu.make_async_copy(src, dst, load_sem.at[i])
        loads[names[i]].start()

    def span_to(o):
        return {"span": (me + o) % spans}

    def sem(kind, o):
        return sems.at[0, kind, o], sems.at[1, kind, o]

    started = []

    def send(src, dst, kind, o, target):
        out = remote(src, dst, *sem(kind, o), target)
        out.start()
        started.append(out)

    def to_peers(kind, src, dst):
        incoming = []
        for o in range(1, spans):
            to, s = (me + o) % spans, (me + spans - o) % spans
            send(src(to), dst(me), kind, o, span_to(o))
            incoming.append(remote(src(to), dst(s), *sem(kind, o), span_to(o)))
        return incoming

    padded[...] = jnp.zeros_like(padded)
    tail[...] = jnp.zeros_like(tail)
    home[bulk:, :] = jnp.zeros_like(home[bulk:, :])
    vhome[:, bulk:, :] = jnp.zeros_like(vhome[:, bulk:, :])
    xs_ref[bulk:, :] = jnp.zeros_like(xs_ref[bulk:, :])
    vs_ref[:, :, bulk:, :] = jnp.zeros_like(vs_ref[:, :, bulk:, :])
    v0_ref[bulk:, :] = jnp.zeros_like(v0_ref[bulk:, :])
    eye = (lax.broadcasted_iota(jnp.int32, (qp, LANES), 0)
           == lax.broadcasted_iota(jnp.int32, (qp, LANES), 1))

    loads["inv"].wait()
    for j in range(zdev):
        padded[:q, :q] = inv_ref[:, j, :]
        inv16[j] = mode_block(padded[...], eye, q)

    for name in ("step", "metric", "adj", "ck", "diff"):
        loads[name].wait()
    for t in range(NSTEP):
        slot = step_ref[t]
        for k in range(2):
            vf[t, k] = ck_ref[slot, k].astype(F32)
    for k in range(2):
        for z in range(zdev):
            vhome[k, :q, z * LANES:(z + 1) * LANES] = vf[0, k, :, z, :]
    for k in range(slabs):
        home[:q, k * LANES:(k + 1) * LANES] = adj_ref[k // zdev, :, k % zdev, :]
    here = metric_ref[...]
    first = jnp.concatenate([here[0:1]] * zdev, axis=1)
    second = jnp.concatenate([here[1:2]] * zdev, axis=1)
    v0 = vhome[0] * first
    v1 = vhome[1] * second
    scales = [None] * 3
    for c in (1, 0, 2):
        lanes = slice(c * wide, (c + 1) * wide)
        moved = transport_block(home[:, lanes], v0, v1, diff_ref, qp)
        home[:, lanes] = moved
        scales[c] = coded_component(moved, snd, c, spans, share, half)
    for k in range(slabs):
        tail[k % spans, k // spans:k // spans + 1, :] = home[bulk:q, k * LANES:(k + 1) * LANES]
    for k in range(2 * zdev):
        for t in range(1, NSTEP):
            tail[k, 1 + t:2 + t, :] = vf[t, k // zdev, bulk:q, k % zdev, :]
    for z in range(zdev):
        tail[z, 1 + NSTEP:2 + NSTEP, :] = vf[0, 1, bulk:q, z, :]
    parts = swap_blocks([tail[g] for g in range(spans)], share)
    for d in range(spans):
        tsnd[d] = jnp.concatenate([parts[d][:5]] + [scales[c][d] for c in range(3)], axis=0)

    pl.semaphore_wait(barrier, spans * planes - 1)

    xpeer = {"plane": (p + 2) % planes}
    cpeer = {"plane": p + 1 - 2 * (p % 2)}
    px = (p + 2) % planes
    pc = p + 1 - 2 * (p % 2)
    pcx = (pc + 2) % planes
    mate = me + 1 - 2 * (me % 2)
    to_mate = {"span": mate}

    def block_of(i):
        return (me + spans - i) % spans if i % 2 == 0 else (mate + spans - i + 1) % spans

    mode_in = {}
    for i in range(2, spans, 2):
        send(inv16.at[p], modes_ref.at[p, me], 0, i, span_to(i))
        mode_in[i] = remote(inv16.at[p], modes_ref.at[p, block_of(i)], *sem(0, i), span_to(i))
    send(inv16.at[p], modes_ref.at[p, me], 0, 1, to_mate)
    mode_in[1] = remote(inv16.at[p], modes_ref.at[p, mate], *sem(0, 1), to_mate)
    for i in range(2, spans, 2):
        s = block_of(i + 1)
        mode_in[i + 1] = remote(modes_ref.at[p, s], modes_ref.at[p, s], *sem(0, i + 1), to_mate)
    fields = [None] * 3
    for c in (1, 0):
        fields[c] = to_peers(4 + c, lambda to: snd.at[c, to], lambda s: rcv.at[c, s])
    tails = to_peers(7, lambda to: tsnd.at[to], lambda s: trc.at[s])
    own = []
    for c in range(3):
        own.append(pltpu.make_async_copy(snd.at[c, me], rcv.at[c, me], local_sem.at[c]))
    own.append(pltpu.make_async_copy(tsnd.at[me], trc.at[me], local_sem.at[3]))
    own += [pltpu.make_async_copy(inv16.at[j], modes_ref.at[j, me], local_sem.at[4 + j]) for j in range(zdev)]
    for c in own:
        c.start()

    speeds = [None] * NSTEP
    for t in range(1, NSTEP):
        parts = swap_blocks([vf[t, k // zdev, :bulk, k % zdev, :] for k in range(2 * zdev)], share)
        for d in range(spans):
            vsnd[t - 1, d] = parts[d].astype(BF16)
        speeds[t] = to_peers(7 + t, lambda to: vsnd.at[t - 1, to], lambda s: vrcv.at[t - 1, s])
    parts = []
    for g in range(spans):
        r = (g % 2) * half
        parts.append(vf[0, 1, r:r + half, g // 2, :])
    parts = swap_blocks(parts, share)
    for d in range(spans):
        wsnd[d] = parts[d].astype(BF16)
    speeds[0] = to_peers(10, lambda to: wsnd.at[to], lambda s: wrc.at[s])
    fields[2] = to_peers(6, lambda to: snd.at[2, to], lambda s: rcv.at[2, s])
    vown = [pltpu.make_async_copy(vsnd.at[t, me], vrcv.at[t, me], local_sem.at[4 + zdev + t]) for t in range(NSTEP - 1)]
    vown.append(pltpu.make_async_copy(wsnd.at[me], wrc.at[me], local_sem.at[3 + zdev + NSTEP]))
    for c in vown:
        c.start()

    later = []
    for i in [2, 1, 4, 6, 3, 5, 7]:
        mode_in[i].wait_recv()
        s = block_of(i)
        if i % 2 == 0:
            send(modes_ref.at[p, s], modes_ref.at[p, s], 0, i + 1, to_mate)
        send(modes_ref.at[p, s], modes_ref.at[p, s], 1, i, xpeer)
        send(modes_ref.at[p, s], modes_ref.at[p, s], 2, i, cpeer)
        later.append((i, s))

    lane = lax.broadcasted_iota(jnp.int32, (1, LANES), 1)
    rolled = pltpu.roll(metric_ref[...], (LANES - me * share) % LANES, 1)
    scale = jnp.where(lane < share, rolled, 0.0)
    k = share
    while k < LANES:
        scale = scale + pltpu.roll(scale, k, 1)
        k *= 2
    first = jnp.concatenate([scale[0:1]] * zdev, axis=1)
    second = jnp.concatenate([scale[1:2]] * zdev, axis=1)
    loads["elem"].wait()
    loads["local"].wait()
    pair = 2 * LANES
    base = p * LANES + me * share
    mode = lax.broadcasted_iota(jnp.int32, (qp, pair), 0)
    near = lax.broadcasted_iota(jnp.int32, (LANES, pair), 0) % share + base
    for piece in range(planes):
        lanes = slice(piece * pair, (piece + 1) * pair)
        for k in range(2):
            pick = jnp.where(local_ref[k:k + 1, lanes] == mode, 1.0, 0.0).astype(BF16)
            picks[piece, k] = jnp.concatenate([pick, pick], axis=0)
            keeps[piece, k] = jnp.where(elem_ref[k:k + 1, lanes] == near, 1.0, 0.0)
    for name in ("basis", "place", "weight"):
        loads[name].wait()

    across, beside, corner = [], [], []
    for i, s in later:
        remote(modes_ref.at[p, s], modes_ref.at[px, s], *sem(1, i), xpeer).wait_recv()
        send(modes_ref.at[px, s], modes_ref.at[px, s], 3, i, cpeer)
        beside.append(remote(modes_ref.at[p, s], modes_ref.at[pc, s], *sem(2, i), cpeer))
        corner.append(remote(modes_ref.at[px, s], modes_ref.at[pcx, s], *sem(3, i), cpeer))

    for c in own:
        c.wait()
    for c in fields[1] + fields[0] + tails:
        c.wait_recv()

    def unpack(c):
        parts = [rcv[c, s].astype(jnp.int32).astype(F32) * trc[s, 5 + c:6 + c, :] for s in range(spans)]
        parts = swap_blocks(parts, share)
        for g in range(spans):
            k, r = c * zdev + g // 2, (g % 2) * half
            xs_ref[r:r + half, k * LANES:(k + 1) * LANES] = parts[g]

    parts = swap_blocks([trc[s] for s in range(spans)], share)
    for k in range(slabs):
        xs_ref[bulk:q, k * LANES:(k + 1) * LANES] = parts[k % spans][k // spans:k // spans + 1]
    for k in range(2 * zdev):
        z = k % zdev
        for t in range(1, NSTEP):
            vs_ref[t - 1, k // zdev, bulk:q, z * LANES:(z + 1) * LANES] = parts[k][1 + t:2 + t]
    for z in range(zdev):
        v0_ref[bulk:q, z * LANES:(z + 1) * LANES] = parts[z][1 + NSTEP:2 + NSTEP]
    unpack(0)
    unpack(1)

    for c in beside + corner:
        c.wait_recv()
    for j in range(zdev):
        for s in range(spans):
            high, low = split(mode_matrix(modes_ref[j, s], eye, q))
            modes_cat[j, s * qp:(s + 1) * qp, :LANES] = high
            modes_cat[j, s * qp:(s + 1) * qp, LANES:2 * LANES] = high
            modes_cat[j, s * qp:(s + 1) * qp, 2 * LANES:] = low

    def step(group, t):
        count = len(group)
        rows = slice(group[0] * qp, (group[-1] + 1) * qp)
        if t:
            v0 = vs_ref[t - 1, 0] * first
            v1 = vs_ref[t - 1, 1] * second
        for c in group:
            x = xs_ref[:, c * wide:(c + 1) * wide]
            if t:
                x = transport_block(x, v0, v1, diff_ref, qp)
            coef[c * qp:(c + 1) * qp, :] = x
        coef[rows, :] = transform(coef[rows, :], basis_ref, False)
        block = lax.broadcasted_iota(jnp.int32, (1, count * LANES), 1) % LANES // share
        gap = jnp.zeros((LANES - qp, count * LANES), BF16)
        for j in range(zdev):
            lanes = slice(j * LANES, (j + 1) * LANES)
            x = jnp.concatenate([coef[c * qp:(c + 1) * qp, lanes] for c in group], axis=1)
            high, low = split(x)
            r = dot(modes_cat[j], jnp.concatenate([high, gap, low, gap, high, gap], axis=0))
            acc = r[:qp]
            for s in range(1, spans):
                acc = jnp.where(block == s, r[s * qp:(s + 1) * qp], acc)
            for i, c in enumerate(group):
                solved[c * qp:(c + 1) * qp, lanes] = acc[:, i * LANES:(i + 1) * LANES]
        y = transform(solved[rows, :], basis_ref, True)
        for i, c in enumerate(group):
            xs_ref[:, c * wide:(c + 1) * wide] = y[i * qp:(i + 1) * qp]

    def unpack_speed(t):
        for c in speeds[t]:
            c.wait_recv()
        parts = swap_blocks([vrcv[t - 1, s].astype(F32) for s in range(spans)], share)
        for k in range(2 * zdev):
            z = k % zdev
            vs_ref[t - 1, k // zdev, :bulk, z * LANES:(z + 1) * LANES] = parts[k]

    one = slice(wide, 2 * wide)

    step((0, 1), 0)
    kept[...] = xs_ref[:, one]

    for c in vown:
        c.wait()
    unpack_speed(1)

    step((0, 1), 1)
    product[...] = xs_ref[:, one] * vs_ref[0, 1]

    unpack_speed(2)

    step((0, 1), 2)

    for c in speeds[0]:
        c.wait_recv()
    parts = swap_blocks([wrc[s].astype(F32) for s in range(spans)], share)
    for g in range(spans):
        z, r = g // 2, (g % 2) * half
        v0_ref[r:r + half, z * LANES:(z + 1) * LANES] = parts[g]
    product[...] += kept[...] * v0_ref[...] + xs_ref[:, one] * vs_ref[1, 1]

    high, low = split(product[...].T)
    left = jnp.concatenate([high, low], axis=1)
    for piece in range(planes):
        got = 0.0
        for k in range(2):
            keep = jnp.concatenate([keeps[piece, k]] * zdev, axis=0)
            got = got + dot(left, picks[piece, k]) * keep
        acc = dot(place_ref[...], jnp.concatenate(split(got), axis=0))
        acc = acc[:, :LANES] + pltpu.roll(acc[:, LANES:], zdev, 0)
        for s in range(spans):
            wall[piece, s] = acc[s * 8:(s + 1) * 8]
    rows = []
    for o in range(1, planes):
        to, s = (p + o) % planes, (p + planes - o) % planes
        send(wall.at[to], rows_in.at[p], 11, o, {"plane": to})
        rows.append(remote(wall.at[to], rows_in.at[s], *sem(11, o), {"plane": to}))
    rown = pltpu.make_async_copy(wall.at[p], rows_in.at[p], local_sem.at[0])
    rown.start()

    scales = [None] * 3
    returned = []
    for c in (0, 1):
        scales[c] = coded_component(xs_ref[:, c * wide:(c + 1) * wide], bsnd, c, spans, share, half)
    rown.wait()
    for c in rows:
        c.wait_recv()
    part[...] = sum(rows_in[s] for s in range(planes))
    walls = to_peers(12, lambda to: part.at[to], lambda s: wrcv.at[s])
    wown = pltpu.make_async_copy(part.at[me], wrcv.at[me], local_sem.at[0])
    wown.start()
    for c in (0, 1):
        returned += to_peers(13 + c, lambda to: bsnd.at[c, to], lambda s: back.at[c, s])

    for c in fields[2]:
        c.wait_recv()
    unpack(2)

    step((2,), 0)
    wown.wait()
    for c in walls:
        c.wait_recv()
    both = sum(wrcv[s] for s in range(spans))
    sums = jnp.concatenate([both[:zdev], both[zdev:]], axis=1)
    weight = weight_ref[:, pl.ds(pl.multiple_of(p * 2 * LANES, 2 * LANES), 2 * LANES)]
    weighted = weight * sums
    weighted_ref[...] = weighted
    sq = weighted * weighted
    square[...] = jnp.sum(sq[:, :LANES] + sq[:, LANES:], axis=0, keepdims=True)
    squares = []
    for a in range(planes):
        for o in range(spans):
            if a or o:
                to = {"plane": (p + a) % planes, "span": (me + o) % spans}
                n = a * spans + o
                out = remote(square, srcv.at[p, me], sqsems.at[0, n], sqsems.at[1, n], to)
                out.start()
                started.append(out)
                squares.append(remote(
                    square, srcv.at[(p + planes - a) % planes, (me + spans - o) % spans],
                    sqsems.at[0, n], sqsems.at[1, n], to))
    srcv[p, me] = square[...]

    step((2,), 1)
    step((2,), 2)

    scales[2] = coded_component(xs_ref[:, 2 * wide:], bsnd, 2, spans, share, half)
    for k in range(slabs):
        tail[k % spans, k // spans:k // spans + 1, :] = xs_ref[bulk:q, k * LANES:(k + 1) * LANES]
    parts = swap_blocks([tail[g] for g in range(spans)], share)
    for d in range(spans):
        tbsnd[d] = jnp.concatenate([parts[d][:5]] + [scales[c][d] for c in range(3)], axis=0)
    returned += to_peers(15, lambda to: bsnd.at[2, to], lambda s: back.at[2, s])
    returned += to_peers(16, lambda to: tbsnd.at[to], lambda s: tback.at[s])
    bown = [pltpu.make_async_copy(bsnd.at[c, me], back.at[c, me], local_sem.at[c]) for c in range(3)]
    bown.append(pltpu.make_async_copy(tbsnd.at[me], tback.at[me], local_sem.at[3]))
    for c in bown:
        c.start()

    for c in squares:
        c.wait_recv()
    for c in bown:
        c.wait()
    for c in returned:
        c.wait_recv()
    for c in started:
        c.wait_send()


def transport_block(x, v0, v1, diff_ref, qp):
    high, low = split(x)
    d = dot(diff_ref[...], jnp.concatenate([high, low, high], axis=0))
    return x + v0 * d[:qp] + v1 * d[qp:]


def coded_component(x, out, c, spans, share, half):
    parts = []
    for g in range(spans):
        z, r = g // 2, (g % 2) * half
        parts.append(x[r:r + half, z * LANES:(z + 1) * LANES])
    parts = swap_blocks(parts, share)
    scales = []
    for d in range(spans):
        whole, scale = coded(parts[d])
        out[c, d] = whole.astype(jnp.int16)
        scales.append(scale)
    return scales


def split(x):
    high = x.astype(BF16)
    return high, (x - high.astype(F32)).astype(BF16)


def dot(a, b, dims=((1,), (0,))):
    return lax.dot_general(a, b, (dims, ((), ())), preferred_element_type=F32)


def transform(x, basis_ref, back):
    high, low = split(x)
    left = jnp.concatenate([high, high, low], axis=1)
    parts = [basis_ref[0], basis_ref[1], basis_ref[0]]
    right = jnp.concatenate(parts, axis=1 if back else 0)
    return dot(left, right, ((1,), (1,)) if back else ((1,), (0,)))


def finish_kernel(spans, planes, zdev, q, count, back, tback, weighted_ref, srcv, out_ref, grad_ref):
    share = LANES // spans
    bulk = q - 1
    half = bulk // 2
    slabs = 3 * zdev
    squares = sum(srcv[a, s] for a in range(planes) for s in range(spans))
    full = jnp.sum(squares, axis=1, keepdims=True)
    grad_ref[...] = weighted_ref[...] * lax.rsqrt(full / count + 1e-06)
    for c in range(3):
        parts = [back[c, s].astype(jnp.int32).astype(F32) * tback[s, 5 + c:6 + c, :] for s in range(spans)]
        parts = swap_blocks(parts, share)
        for g in range(spans):
            r = (g % 2) * half
            out_ref[c, r:r + half, g // 2, :] = parts[g]
    parts = swap_blocks([tback[s] for s in range(spans)], share)
    for k in range(slabs):
        out_ref[k // zdev, bulk:q, k % zdev, :] = parts[k % spans][k // spans:k // spans + 1]


def halves(table):
    high = table.astype(np.float32).astype(ml_dtypes.bfloat16)
    low = (table - high.astype(np.float64)).astype(np.float32).astype(ml_dtypes.bfloat16)
    return np.stack([high, low])


def tables(spans, zdev, q, qp):
    share = LANES // spans
    fourier = fourier_table(spans * zdev)
    order = np.array([s * zdev + z for z in range(zdev) for s in range(spans)])
    basis = np.kron(fourier[order][:, order].T, np.eye(share))
    side = P_SIZE + 1
    matrix = chebyshev_matrix(P_SIZE)
    diff = np.zeros((2 * qp, qp))
    diff[:q, :q] = np.kron(matrix, np.eye(side))
    diff[qp:qp + q, :q] = np.kron(np.eye(side), matrix)
    place = np.zeros((spans * 8, zdev * LANES), ml_dtypes.bfloat16)
    for s in range(spans):
        for z in range(zdev):
            at = z * LANES + s * share
            place[s * 8 + z, at:at + share] = 1.0
    high, low = halves(diff)
    diff = np.concatenate([high, high, low], axis=1)
    place = np.concatenate([place, place], axis=1)
    return halves(basis), diff, place


def vmem(n):
    return [pl.BlockSpec(memory_space=pltpu.VMEM)] * n


def kernels_on_device(spans, planes, adjoint, checkpoints, checkpoint_step, metric,
                      helmholtz_inverse, wall_element, wall_local, wall_weight):
    _, zdev, q, _ = adjoint.shape
    wall_count = wall_element.shape[0]
    qp = -(-q // 16) * 16
    bulk, wide = q - 1, zdev * LANES
    half = bulk // 2
    shape = jax.ShapeDtypeStruct
    basis, diff, place = tables(spans, zdev, q, qp)
    basis, diff, place = jnp.asarray(basis), jnp.asarray(diff), jnp.asarray(place)
    operands = (checkpoint_step, adjoint.transpose(0, 2, 1, 3), checkpoints.transpose(0, 1, 3, 2, 4),
                helmholtz_inverse.transpose(1, 0, 2), metric, wall_element.T, wall_local.T,
                wall_weight, basis, diff, place)
    landing = [pltpu.SMEM(checkpoint_step.shape, jnp.int32)]
    landing += [pltpu.VMEM(a.shape, a.dtype) for a in operands[1:]]
    back, tback, weighted, squares = pl.pallas_call(
        functools.partial(step_kernel, spans, planes, zdev, q, qp),
        out_shape=(shape((3, spans, half, LANES), jnp.int16), shape((spans, 8, LANES), F32),
                   shape((zdev, wall_count // planes), F32),
                   shape((planes, spans, 1, LANES), F32)),
        in_specs=[pl.BlockSpec(memory_space=pl.ANY)] * len(operands),
        out_specs=tuple(vmem(4)),
        scratch_shapes=landing + [
            pltpu.VMEM((qp, 3 * wide), F32),
            pltpu.VMEM((2, qp, wide), F32),
            pltpu.VMEM((NSTEP, 2, q, zdev, LANES), F32),
            pltpu.VMEM((qp, 3 * wide), F32),
            pltpu.VMEM((NSTEP - 1, 2, qp, wide), F32),
            pltpu.VMEM((qp, wide), F32),
            pltpu.VMEM((qp, LANES), F32),
            pltpu.VMEM((zdev, qp, LANES), jnp.int16),
            pltpu.VMEM((zdev, spans, qp, LANES), jnp.int16),
            pltpu.VMEM((spans, 8, LANES), F32),
            pltpu.VMEM((3, spans, half, LANES), jnp.int16),
            pltpu.VMEM((spans, 8, LANES), F32),
            pltpu.VMEM((3, spans, half, LANES), jnp.int16),
            pltpu.VMEM((spans, 8, LANES), F32),
            pltpu.VMEM((NSTEP - 1, spans, bulk, LANES), BF16),
            pltpu.VMEM((NSTEP - 1, spans, bulk, LANES), BF16),
            pltpu.VMEM((spans, half, LANES), BF16),
            pltpu.VMEM((spans, half, LANES), BF16),
            pltpu.VMEM((3 * qp, wide), F32),
            pltpu.VMEM((3 * qp, wide), F32),
            pltpu.VMEM((qp, wide), F32),
            pltpu.VMEM((qp, wide), F32),
            pltpu.VMEM((zdev, spans * qp, 3 * LANES), BF16),
            pltpu.VMEM((3, spans, half, LANES), jnp.int16),
            pltpu.VMEM((spans, 8, LANES), F32),
            pltpu.VMEM((planes, 2, 2 * qp, 2 * LANES), BF16),
            pltpu.VMEM((planes, 2, LANES, 2 * LANES), F32),
            pltpu.VMEM((planes, spans, 8, LANES), F32),
            pltpu.VMEM((planes, spans, 8, LANES), F32),
            pltpu.VMEM((spans, 8, LANES), F32),
            pltpu.VMEM((spans, 8, LANES), F32),
            pltpu.VMEM((1, LANES), F32),
            pltpu.SemaphoreType.DMA((2, 17, spans)),
            pltpu.SemaphoreType.DMA((2, planes * spans)),
            pltpu.SemaphoreType.DMA((len(operands),)),
            pltpu.SemaphoreType.DMA((4 + zdev + NSTEP,)),
        ],
        compiler_params=pltpu.CompilerParams(collective_id=0, has_side_effects=True),
        name="steps",
    )(*operands)
    field, gradient = pl.pallas_call(
        functools.partial(finish_kernel, spans, planes, zdev, q, float(spans * zdev * wall_count)),
        out_shape=(shape((3, q, zdev, LANES), F32), shape((zdev, wall_count // planes), F32)),
        in_specs=vmem(4),
        out_specs=tuple(vmem(2)),
        name="finish",
    )(back, tback, weighted, squares)
    return field.transpose(0, 2, 1, 3), gradient


def chosen(spans, planes, *args):
    zdev, q, elems = args[0].shape[1:]
    walls = args[5].shape[0]
    fits = (
        elems == LANES and spans == 2 * zdev and planes == zdev == 4
        and walls == planes * 2 * LANES and q % 16 == 1 and q < LANES
    )
    if fits:
        return kernels_on_device(spans, planes, *args)
    return on_device(*args)


def solution(mesh):
    placed = (
        P(None, "span", None, "plane"),
        P(None, None, "span", None, "plane"),
        P(),
        P(None, "plane"),
        P("span", None, None),
        P(),
        P(),
        P("span", None),
    )
    return jax.shard_map(
        functools.partial(chosen, mesh.shape["span"], mesh.shape["plane"]),
        mesh=mesh,
        in_specs=placed,
        out_specs=(P(None, "span", None, "plane"), P("span", "plane")),
        check_vma=False,
    )
```

```python
import functools

import jax
import jax.numpy as jnp
import ml_dtypes
import numpy as np
from jax import lax
from jax.experimental import pallas as pl
from jax.experimental.pallas import tpu as pltpu
from jax.sharding import PartitionSpec as P

P_SIZE = 8
NSTEP = 3


HIGHEST = lax.Precision.HIGHEST


def chebyshev_matrix(degree):
    points = np.arange(degree + 1)
    abscissa = np.cos(np.pi * points / degree)
    signed = np.where((points == 0) | (points == degree), 2.0, 1.0) * (-1.0) ** points
    spacing = abscissa[:, None] - abscissa[None, :] + np.eye(degree + 1)
    matrix = signed[:, None] / signed[None, :] / spacing
    return matrix - np.eye(degree + 1) * np.sum(matrix, axis=1)[:, None]


def fourier_table(length):
    row_index = np.arange(length)[:, None]
    column = np.arange(length)[None, :]
    wavenumber = (row_index + 1) // 2
    phase_angle = 2.0 * np.pi * wavenumber * column / length
    parity = row_index % 2
    base_rows = np.where(
        row_index == 0, 1.0, np.where(parity == 1, np.cos(phase_angle), np.sin(phase_angle))
    )
    row_scale = np.where(
        (row_index == 0) | (row_index == length - 1), 1.0 / np.sqrt(length), np.sqrt(2.0 / length)
    )
    return base_rows * row_scale


def transport(field_data, velocity, metric):
    side_nodes = P_SIZE + 1
    matrix = jnp.asarray(chebyshev_matrix(P_SIZE), jnp.float32)
    shaped = field_data.reshape(
        field_data.shape[0], field_data.shape[1], side_nodes, side_nodes, field_data.shape[3]
    )
    first_dir = jnp.einsum("ai,czibe->czabe", matrix, shaped, precision=HIGHEST).reshape(
        field_data.shape
    )
    second_dir = jnp.einsum("bi,czaie->czabe", matrix, shaped, precision=HIGHEST).reshape(
        field_data.shape
    )
    speed_data = velocity.astype(jnp.float32)
    return (
        field_data
        + speed_data[0] * (metric[0] * first_dir)
        + speed_data[1] * (metric[1] * second_dir)
    )


def forward_modes(gathered):
    basis_table = jnp.asarray(fourier_table(gathered.shape[1]), jnp.float32)
    return jnp.einsum("jz,czqe->cjqe", basis_table, gathered, precision=HIGHEST)


def backward_planes(solved):
    basis_table = jnp.asarray(fourier_table(solved.shape[1]), jnp.float32)
    return jnp.einsum("jz,cjqe->czqe", basis_table, solved, precision=HIGHEST)


def solve_modes(inverse_block, coefficients):
    return jnp.einsum("jqr,cjre->cjqe", inverse_block, coefficients, precision=HIGHEST)


def to_plane_layout(point_data):
    return lax.all_to_all(point_data, "span", split_axis=1, concat_axis=3, tiled=True)


def wall_terms(field_one, speed_one, flat_index, inside, wall_count):
    rows = field_one.shape[0]
    values = jnp.take(field_one.reshape(rows, -1), flat_index, axis=1)
    speeds = jnp.take(speed_one.reshape(rows, -1), flat_index, axis=1).astype(jnp.float32)
    product = jnp.where(inside, values * speeds, 0.0).reshape(rows, wall_count, 2)
    return jnp.sum(product, axis=2)


def on_device(
    adjoint,
    checkpoints,
    checkpoint_step,
    metric,
    helmholtz_inverse,
    wall_element,
    wall_local,
    wall_weight,
):
    planes_dev = adjoint.shape[1]
    elems_dev = adjoint.shape[3]
    wall_count = wall_element.shape[0]
    span_count = lax.axis_size("span")
    share = elems_dev // span_count
    all_modes = lax.all_gather(helmholtz_inverse, "span", axis=0, tiled=True)
    offset = lax.axis_index("plane") * elems_dev
    local_element = wall_element - offset
    inside = ((local_element >= 0) & (local_element < elems_dev)).reshape(-1)
    flat_index = (wall_local * elems_dev + jnp.clip(local_element, 0, elems_dev - 1)).reshape(-1)
    velocity = jnp.stack([
        lax.dynamic_index_in_dim(checkpoints, checkpoint_step[s], 0, keepdims=False)
        for s in range(NSTEP)
    ])
    velocity = lax.all_to_all(velocity, "span", split_axis=4, concat_axis=2, tiled=True)
    field = lax.all_to_all(adjoint, "span", split_axis=3, concat_axis=1, tiled=True)
    scale = lax.dynamic_slice_in_dim(metric, lax.axis_index("span") * share, share, 1)
    product = 0.0
    for substep in range(NSTEP):
        advected = transport(field, velocity[substep], scale)
        field = backward_planes(solve_modes(all_modes, forward_modes(advected)))
        product = product + field[1] * velocity[substep, 1].astype(jnp.float32)
    both = to_plane_layout(jnp.concatenate([field, product[None]], axis=0))
    gathered = jnp.take(both[3].reshape(planes_dev, -1), flat_index, axis=1)
    partial_sum = jnp.where(inside, gathered, 0.0).reshape(planes_dev, wall_count, 2).sum(axis=2)
    weighted = wall_weight * partial_sum
    grad_share = lax.psum_scatter(weighted, "plane", scatter_dimension=1, tiled=True)
    square_total = lax.psum(jnp.sum(grad_share * grad_share), ("span", "plane"))
    inverse_rms = lax.rsqrt(square_total / (planes_dev * span_count * wall_count) + 1e-06)
    return (both[:3], grad_share * inverse_rms)


MESH = pl.DeviceIdType.MESH
F32 = jnp.float32
BF16 = jnp.bfloat16
LANES = 128
NKINDS = 18


def swap_blocks(parts, share):
    count = len(parts)
    width = count * share
    lane = lax.broadcasted_iota(jnp.int32, parts[0].shape, 1)
    k = count // 2
    while k:
        upper = (lane // (k * share)) % 2 == 1
        new = list(parts)
        for i in range(count):
            if (i // k) % 2 == 0:
                a, b = parts[i], parts[i + k]
                new[i] = jnp.where(upper, pltpu.roll(b, k * share, 1), a)
                new[i + k] = jnp.where(upper, b, pltpu.roll(a, width - k * share, 1))
        parts = new
        k //= 2
    return parts


def coded(x):
    top = jnp.maximum(jnp.max(jnp.abs(x), axis=0, keepdims=True), 1e-30)
    return jnp.round(x * (32767.0 / top)).astype(jnp.int32), top * (1.0 / 32767.0)


def remote(src, dst, sem_out, sem_in, target):
    return pltpu.make_async_remote_copy(
        src_ref=src, dst_ref=dst, send_sem=sem_out, recv_sem=sem_in,
        device_id=target, device_id_type=MESH,
    )


def mode_block(x, eye, q):
    diag = jnp.sum(jnp.where(eye, x, 0.0), axis=0, keepdims=True)
    off = jnp.where(eye, 0.0, x)
    row = lax.broadcasted_iota(jnp.int32, x.shape, 0)
    power = power_of(jnp.max(jnp.abs(off), axis=0, keepdims=True))
    power_d = power_of(jnp.abs(diag))
    unit = diag * (32767.0 * jnp.exp2(-power_d))
    high = jnp.round(unit)
    low = jnp.round((unit - high) * 32767.0)
    whole = jnp.round(off * (32767.0 * jnp.exp2(-power)))
    for i, extra in enumerate((power, power_d, high, low)):
        whole = jnp.where(row == q + i, extra, whole)
    return whole.astype(jnp.int32).astype(jnp.int16)


def power_of(top):
    return jnp.ceil(jnp.log2(jnp.maximum(top, 1e-30)))


def mode_matrix(block, eye, q):
    x = block.astype(jnp.int32).astype(F32)
    scale = jnp.exp2(x[q:q + 1]) * (1.0 / 32767.0)
    diag = (x[q + 2:q + 3] + x[q + 3:q + 4] * (1.0 / 32767.0)) * (jnp.exp2(x[q + 1:q + 2]) * (1.0 / 32767.0))
    row = lax.broadcasted_iota(jnp.int32, x.shape, 0)
    return jnp.where(eye, diag, jnp.where(row < q, x, 0.0) * scale)


def step_kernel(spans, planes, zdev, q, qp,
                step_h, adj_h, ck_h, inv_h, metric_h, elem_h, local_h, weight_h, basis_h, diff_h, place_h,
                back, tback, weighted_ref, srcv,
                step_ref, adj_ref, ck_ref, inv_ref, metric_ref, elem_ref, local_ref, weight_ref,
                basis_ref, diff_ref, place_ref,
                home, vhome, vf, xs_ref, vs_ref, v0_ref, padded, inv16, modes_ref, tail,
                snd, tsnd, rcv, trc, vsnd, vrcv, wsnd, wrc,
                coef, solved, product, kept, modes_cat, bsnd, tbsnd,
                picks, keeps, wall, rows_in, part, wrcv, square, sems, load_sem, local_sem):
    share = LANES // spans
    me, p = lax.axis_index("span"), lax.axis_index("plane")
    bulk = q - 1
    half = bulk // 2
    slabs = 3 * zdev
    wide = zdev * LANES

    barrier = pltpu.get_barrier_semaphore()
    for a in range(planes):
        for o in range(spans):
            if a or o:
                pl.semaphore_signal(
                    barrier, 1, device_id={"plane": (p + a) % planes, "span": (me + o) % spans},
                    device_id_type=MESH)
    names = ("inv", "step", "metric", "adj", "ck", "diff", "elem", "local", "place", "basis", "weight")
    pairs = ((inv_h, inv_ref), (step_h, step_ref), (metric_h, metric_ref), (adj_h, adj_ref), (ck_h, ck_ref),
             (diff_h, diff_ref), (elem_h, elem_ref), (local_h, local_ref), (place_h, place_ref),
             (basis_h, basis_ref), (weight_h, weight_ref))
    loads = {}
    for i, (src, dst) in enumerate(pairs):
        loads[names[i]] = pltpu.make_async_copy(src, dst, load_sem.at[i])
        loads[names[i]].start()

    def span_to(o):
        return {"span": (me + o) % spans}

    mate = me + 1 - 2 * (me % 2)
    to_mate = {"span": mate}
    most = slice(0, spans - 1)

    started = []

    def send(src, dst, kind, recv, target):
        remote(src, dst, sems.at[0, kind], sems.at[1, recv], target).start()

    def arrival(dst, recv):
        return remote(dst, dst, sems.at[0, 0], sems.at[1, recv], to_mate)

    def sent(kind, whole):
        started.append(remote(whole, whole, sems.at[0, kind], sems.at[1, 0], to_mate))

    def to_peers(kind, src, dst, whole):
        for o in range(1, spans):
            send(src((me + o) % spans), dst(me), kind, kind, span_to(o))
        sent(kind, whole)
        return arrival(whole, kind)

    padded[...] = jnp.zeros_like(padded)
    tail[...] = jnp.zeros_like(tail)
    home[bulk:, :] = jnp.zeros_like(home[bulk:, :])
    vhome[:, bulk:, :] = jnp.zeros_like(vhome[:, bulk:, :])
    xs_ref[bulk:, :] = jnp.zeros_like(xs_ref[bulk:, :])
    vs_ref[:, :, bulk:, :] = jnp.zeros_like(vs_ref[:, :, bulk:, :])
    v0_ref[bulk:, :] = jnp.zeros_like(v0_ref[bulk:, :])
    eye = (lax.broadcasted_iota(jnp.int32, (qp, LANES), 0)
           == lax.broadcasted_iota(jnp.int32, (qp, LANES), 1))

    loads["inv"].wait()
    for j in range(zdev):
        padded[:q, :q] = inv_ref[:, j, :]
        inv16[j] = mode_block(padded[...], eye, q)

    pl.semaphore_wait(barrier, spans * planes - 1)

    xpeer = {"plane": (p + 2) % planes}
    cpeer = {"plane": p + 1 - 2 * (p % 2)}
    px = (p + 2) % planes
    pc = p + 1 - 2 * (p % 2)
    pcx = (pc + 2) % planes
    single = NKINDS

    def block_of(i):
        return (me + spans - i) % spans if i % 2 == 0 else (mate + spans - i + 1) % spans

    for i in range(2, spans, 2):
        send(inv16.at[p], modes_ref.at[p, me], 0, single + i, span_to(i))
    send(inv16.at[p], modes_ref.at[p, me], 0, single + 1, to_mate)
    own = [pltpu.make_async_copy(inv16.at[j], modes_ref.at[j, me], local_sem.at[4 + j]) for j in range(zdev)]
    for c in own:
        c.start()
    for kind in range(4):
        sent(kind, modes_ref.at[0, most])

    def relay(i):
        s = block_of(i)
        block = modes_ref.at[p, s]
        arrival(block, single + i).wait_recv()
        if i % 2 == 0:
            send(block, block, 0, single + i + 1, to_mate)
        send(block, block, 1, single + spans + i, xpeer)
        send(block, block, 2, 2, cpeer)

    def relay_across(i):
        block = modes_ref.at[px, block_of(i)]
        arrival(block, single + spans + i).wait_recv()
        send(block, block, 3, 3, cpeer)

    for name in ("step", "metric", "adj", "ck", "diff"):
        loads[name].wait()
    for t in range(NSTEP):
        slot = step_ref[t]
        for k in range(2):
            vf[t, k] = ck_ref[slot, k].astype(F32)
    for k in range(2):
        for z in range(zdev):
            vhome[k, :q, z * LANES:(z + 1) * LANES] = vf[0, k, :, z, :]
    for k in range(slabs):
        home[:q, k * LANES:(k + 1) * LANES] = adj_ref[k // zdev, :, k % zdev, :]
    here = metric_ref[...]
    first = jnp.concatenate([here[0:1]] * zdev, axis=1)
    second = jnp.concatenate([here[1:2]] * zdev, axis=1)
    v0 = vhome[0] * first
    v1 = vhome[1] * second
    scales = [None] * 3
    for c in (1, 0, 2):
        lanes = slice(c * wide, (c + 1) * wide)
        moved = transport_block(home[:, lanes], v0, v1, diff_ref, qp)
        home[:, lanes] = moved
        scales[c] = coded_component(moved, snd, c, spans, share, half)
    for k in range(slabs):
        tail[k % spans, k // spans:k // spans + 1, :] = home[bulk:q, k * LANES:(k + 1) * LANES]
    for k in range(2 * zdev):
        for t in range(1, NSTEP):
            tail[k, 1 + t:2 + t, :] = vf[t, k // zdev, bulk:q, k % zdev, :]
    for z in range(zdev):
        tail[z, 1 + NSTEP:2 + NSTEP, :] = vf[0, 1, bulk:q, z, :]
    parts = swap_blocks([tail[g] for g in range(spans)], share)
    for d in range(spans):
        tsnd[d] = jnp.concatenate([parts[d][:5]] + [scales[c][d] for c in range(3)], axis=0)

    fields = [None] * 3

    def send_field(c):
        fields[c] = to_peers(4 + c, lambda to: snd.at[c, to], lambda s: rcv.at[c, s], rcv.at[c, most])

    speeds = [None] * NSTEP

    def send_speed(t):
        parts = swap_blocks([vf[t, k // zdev, :bulk, k % zdev, :] for k in range(2 * zdev)], share)
        for d in range(spans):
            vsnd[t - 1, d] = parts[d].astype(BF16)
        speeds[t] = to_peers(7 + t, lambda to: vsnd.at[t - 1, to], lambda s: vrcv.at[t - 1, s], vrcv.at[t - 1, most])

    relay(2)
    send_field(1)
    relay(1)
    relay(4)
    send_field(0)
    tails = to_peers(7, lambda to: tsnd.at[to], lambda s: trc.at[s], trc.at[most])
    send_speed(1)
    relay(6)
    relay(3)
    send_speed(2)
    relay(5)
    relay(7)
    relay_across(2)
    parts = []
    for g in range(spans):
        r = (g % 2) * half
        parts.append(vf[0, 1, r:r + half, g // 2, :])
    parts = swap_blocks(parts, share)
    for d in range(spans):
        wsnd[d] = parts[d].astype(BF16)
    speeds[0] = to_peers(10, lambda to: wsnd.at[to], lambda s: wrc.at[s], wrc.at[most])
    send_field(2)
    for c in range(3):
        own.append(pltpu.make_async_copy(snd.at[c, me], rcv.at[c, me], local_sem.at[c]))
    own.append(pltpu.make_async_copy(tsnd.at[me], trc.at[me], local_sem.at[3]))
    vown = [pltpu.make_async_copy(vsnd.at[t, me], vrcv.at[t, me], local_sem.at[4 + zdev + t]) for t in range(NSTEP - 1)]
    vown.append(pltpu.make_async_copy(wsnd.at[me], wrc.at[me], local_sem.at[3 + zdev + NSTEP]))
    for c in own[zdev:] + vown:
        c.start()
    for i in (1, 4, 6):
        relay_across(i)

    lane = lax.broadcasted_iota(jnp.int32, (1, LANES), 1)
    rolled = pltpu.roll(metric_ref[...], (LANES - me * share) % LANES, 1)
    scale = jnp.where(lane < share, rolled, 0.0)
    k = share
    while k < LANES:
        scale = scale + pltpu.roll(scale, k, 1)
        k *= 2
    first = jnp.concatenate([scale[0:1]] * zdev, axis=1)
    second = jnp.concatenate([scale[1:2]] * zdev, axis=1)
    loads["elem"].wait()
    loads["local"].wait()
    pair = 2 * LANES
    base = p * LANES + me * share
    mode = lax.broadcasted_iota(jnp.int32, (qp, pair), 0)
    near = lax.broadcasted_iota(jnp.int32, (LANES, pair), 0) % share + base
    for piece in range(planes):
        lanes = slice(piece * pair, (piece + 1) * pair)
        for k in range(2):
            pick = jnp.where(local_ref[k:k + 1, lanes] == mode, 1.0, 0.0).astype(BF16)
            picks[piece, k] = jnp.concatenate([pick, pick], axis=0)
            keeps[piece, k] = jnp.where(elem_ref[k:k + 1, lanes] == near, 1.0, 0.0)
    for name in ("basis", "place", "weight"):
        loads[name].wait()

    for i in (3, 5, 7):
        relay_across(i)

    for c in own:
        c.wait()
    for c in (fields[1], fields[0], tails):
        c.wait_recv()

    def unpack(c):
        parts = [rcv[c, s].astype(jnp.int32).astype(F32) * trc[s, 5 + c:6 + c, :] for s in range(spans)]
        parts = swap_blocks(parts, share)
        for g in range(spans):
            k, r = c * zdev + g // 2, (g % 2) * half
            xs_ref[r:r + half, k * LANES:(k + 1) * LANES] = parts[g]

    parts = swap_blocks([trc[s] for s in range(spans)], share)
    for k in range(slabs):
        xs_ref[bulk:q, k * LANES:(k + 1) * LANES] = parts[k % spans][k // spans:k // spans + 1]
    for k in range(2 * zdev):
        z = k % zdev
        for t in range(1, NSTEP):
            vs_ref[t - 1, k // zdev, bulk:q, z * LANES:(z + 1) * LANES] = parts[k][1 + t:2 + t]
    for z in range(zdev):
        v0_ref[bulk:q, z * LANES:(z + 1) * LANES] = parts[z][1 + NSTEP:2 + NSTEP]
    unpack(0)
    unpack(1)

    for kind, plane in ((2, pc), (3, pcx)):
        arrival(modes_ref.at[plane, most], kind).wait_recv()
    for j in range(zdev):
        for s in range(spans):
            high, low = split(mode_matrix(modes_ref[j, s], eye, q))
            modes_cat[j, s * qp:(s + 1) * qp, :LANES] = high
            modes_cat[j, s * qp:(s + 1) * qp, LANES:2 * LANES] = high
            modes_cat[j, s * qp:(s + 1) * qp, 2 * LANES:] = low

    def step(group, t):
        count = len(group)
        rows = slice(group[0] * qp, (group[-1] + 1) * qp)
        if t:
            v0 = vs_ref[t - 1, 0] * first
            v1 = vs_ref[t - 1, 1] * second
        for c in group:
            x = xs_ref[:, c * wide:(c + 1) * wide]
            if t:
                x = transport_block(x, v0, v1, diff_ref, qp)
            coef[c * qp:(c + 1) * qp, :] = x
        coef[rows, :] = transform(coef[rows, :], basis_ref, False)
        block = lax.broadcasted_iota(jnp.int32, (1, count * LANES), 1) % LANES // share
        gap = jnp.zeros((LANES - qp, count * LANES), BF16)
        for j in range(zdev):
            lanes = slice(j * LANES, (j + 1) * LANES)
            x = jnp.concatenate([coef[c * qp:(c + 1) * qp, lanes] for c in group], axis=1)
            high, low = split(x)
            r = dot(modes_cat[j], jnp.concatenate([high, gap, low, gap, high, gap], axis=0))
            acc = r[:qp]
            for s in range(1, spans):
                acc = jnp.where(block == s, r[s * qp:(s + 1) * qp], acc)
            for i, c in enumerate(group):
                solved[c * qp:(c + 1) * qp, lanes] = acc[:, i * LANES:(i + 1) * LANES]
        y = transform(solved[rows, :], basis_ref, True)
        for i, c in enumerate(group):
            xs_ref[:, c * wide:(c + 1) * wide] = y[i * qp:(i + 1) * qp]

    def unpack_speed(t):
        speeds[t].wait_recv()
        parts = swap_blocks([vrcv[t - 1, s].astype(F32) for s in range(spans)], share)
        for k in range(2 * zdev):
            z = k % zdev
            vs_ref[t - 1, k // zdev, :bulk, z * LANES:(z + 1) * LANES] = parts[k]

    one = slice(wide, 2 * wide)

    step((0, 1), 0)
    kept[...] = xs_ref[:, one]

    for c in vown:
        c.wait()
    unpack_speed(1)

    step((0, 1), 1)
    product[...] = xs_ref[:, one] * vs_ref[0, 1]

    unpack_speed(2)

    step((0, 1), 2)

    speeds[0].wait_recv()
    parts = swap_blocks([wrc[s].astype(F32) for s in range(spans)], share)
    for g in range(spans):
        z, r = g // 2, (g % 2) * half
        v0_ref[r:r + half, z * LANES:(z + 1) * LANES] = parts[g]
    product[...] += kept[...] * v0_ref[...] + xs_ref[:, one] * vs_ref[1, 1]

    high, low = split(product[...].T)
    left = jnp.concatenate([high, low], axis=1)
    for piece in range(planes):
        got = 0.0
        for k in range(2):
            keep = jnp.concatenate([keeps[piece, k]] * zdev, axis=0)
            got = got + dot(left, picks[piece, k]) * keep
        acc = dot(place_ref[...], jnp.concatenate(split(got), axis=0))
        acc = acc[:, :LANES] + pltpu.roll(acc[:, LANES:], zdev, 0)
        for s in range(spans):
            wall[piece, s] = acc[s * 8:(s + 1) * 8]
    for o in range(1, planes):
        to = (p + o) % planes
        send(wall.at[to], rows_in.at[p], 11, 11, {"plane": to})
    sent(11, wall.at[slice(0, planes - 1)])
    rown = pltpu.make_async_copy(wall.at[p], rows_in.at[p], local_sem.at[0])
    rown.start()

    scales = [None] * 3
    returned = []
    for c in (0, 1):
        scales[c] = coded_component(xs_ref[:, c * wide:(c + 1) * wide], bsnd, c, spans, share, half)
        returned.append(to_peers(13 + c, lambda to: bsnd.at[c, to], lambda s: back.at[c, s], back.at[c, most]))

    fields[2].wait_recv()
    unpack(2)

    step((2,), 0)

    rown.wait()
    arrival(rows_in.at[slice(0, planes - 1)], 11).wait_recv()
    part[...] = sum(rows_in[s] for s in range(planes))
    walls = to_peers(12, lambda to: part.at[to], lambda s: wrcv.at[s], wrcv.at[most])
    wown = pltpu.make_async_copy(part.at[me], wrcv.at[me], local_sem.at[0])
    wown.start()

    step((2,), 1)

    wown.wait()
    walls.wait_recv()
    both = sum(wrcv[s] for s in range(spans))
    sums = jnp.concatenate([both[:zdev], both[zdev:]], axis=1)
    weight = weight_ref[:, pl.ds(pl.multiple_of(p * 2 * LANES, 2 * LANES), 2 * LANES)]
    weighted = weight * sums
    weighted_ref[...] = weighted
    sq = weighted * weighted
    square[...] = jnp.sum(sq[:, :LANES] + sq[:, LANES:], axis=0, keepdims=True)
    where = p * spans + me
    for a in range(planes):
        for o in range(spans):
            if a or o:
                send(square, srcv.at[where], 17, 17, {"plane": (p + a) % planes, "span": (me + o) % spans})
    others = srcv.at[slice(0, planes * spans - 1)]
    sent(17, others)
    srcv[where] = square[...]

    step((2,), 2)

    scales[2] = coded_component(xs_ref[:, 2 * wide:], bsnd, 2, spans, share, half)
    for k in range(slabs):
        tail[k % spans, k // spans:k // spans + 1, :] = xs_ref[bulk:q, k * LANES:(k + 1) * LANES]
    parts = swap_blocks([tail[g] for g in range(spans)], share)
    for d in range(spans):
        tbsnd[d] = jnp.concatenate([parts[d][:5]] + [scales[c][d] for c in range(3)], axis=0)
    returned.append(to_peers(15, lambda to: bsnd.at[2, to], lambda s: back.at[2, s], back.at[2, most]))
    returned.append(to_peers(16, lambda to: tbsnd.at[to], lambda s: tback.at[s], tback.at[most]))
    bown = [pltpu.make_async_copy(bsnd.at[c, me], back.at[c, me], local_sem.at[c]) for c in range(3)]
    bown.append(pltpu.make_async_copy(tbsnd.at[me], tback.at[me], local_sem.at[3]))
    for c in bown:
        c.start()

    arrival(others, 17).wait_recv()
    for c in bown:
        c.wait()
    for c in returned:
        c.wait_recv()
    for c in started:
        c.wait_send()


def transport_block(x, v0, v1, diff_ref, qp):
    high, low = split(x)
    d = dot(diff_ref[...], jnp.concatenate([high, low, high], axis=0))
    return x + v0 * d[:qp] + v1 * d[qp:]


def coded_component(x, out, c, spans, share, half):
    parts = []
    for g in range(spans):
        z, r = g // 2, (g % 2) * half
        parts.append(x[r:r + half, z * LANES:(z + 1) * LANES])
    parts = swap_blocks(parts, share)
    scales = []
    for d in range(spans):
        whole, scale = coded(parts[d])
        out[c, d] = whole.astype(jnp.int16)
        scales.append(scale)
    return scales


def split(x):
    high = x.astype(BF16)
    return high, (x - high.astype(F32)).astype(BF16)


def dot(a, b, dims=((1,), (0,))):
    return lax.dot_general(a, b, (dims, ((), ())), preferred_element_type=F32)


def transform(x, basis_ref, back):
    high, low = split(x)
    left = jnp.concatenate([high, high, low], axis=1)
    parts = [basis_ref[0], basis_ref[1], basis_ref[0]]
    right = jnp.concatenate(parts, axis=1 if back else 0)
    return dot(left, right, ((1,), (1,)) if back else ((1,), (0,)))


def finish_kernel(spans, planes, zdev, q, count, back, tback, weighted_ref, srcv, out_ref, grad_ref):
    share = LANES // spans
    bulk = q - 1
    half = bulk // 2
    slabs = 3 * zdev
    squares = sum(srcv[n] for n in range(planes * spans))
    full = jnp.sum(squares, axis=1, keepdims=True)
    grad_ref[...] = weighted_ref[...] * lax.rsqrt(full / count + 1e-06)
    for c in range(3):
        parts = [back[c, s].astype(jnp.int32).astype(F32) * tback[s, 5 + c:6 + c, :] for s in range(spans)]
        parts = swap_blocks(parts, share)
        for g in range(spans):
            r = (g % 2) * half
            out_ref[c, r:r + half, g // 2, :] = parts[g]
    parts = swap_blocks([tback[s] for s in range(spans)], share)
    for k in range(slabs):
        out_ref[k // zdev, bulk:q, k % zdev, :] = parts[k % spans][k // spans:k // spans + 1]


def halves(table):
    high = table.astype(np.float32).astype(ml_dtypes.bfloat16)
    low = (table - high.astype(np.float64)).astype(np.float32).astype(ml_dtypes.bfloat16)
    return np.stack([high, low])


def tables(spans, zdev, q, qp):
    share = LANES // spans
    fourier = fourier_table(spans * zdev)
    order = np.array([s * zdev + z for z in range(zdev) for s in range(spans)])
    basis = np.kron(fourier[order][:, order].T, np.eye(share))
    side = P_SIZE + 1
    matrix = chebyshev_matrix(P_SIZE)
    diff = np.zeros((2 * qp, qp))
    diff[:q, :q] = np.kron(matrix, np.eye(side))
    diff[qp:qp + q, :q] = np.kron(np.eye(side), matrix)
    place = np.zeros((spans * 8, zdev * LANES), ml_dtypes.bfloat16)
    for s in range(spans):
        for z in range(zdev):
            at = z * LANES + s * share
            place[s * 8 + z, at:at + share] = 1.0
    high, low = halves(diff)
    diff = np.concatenate([high, high, low], axis=1)
    place = np.concatenate([place, place], axis=1)
    return halves(basis), diff, place


def vmem(n):
    return [pl.BlockSpec(memory_space=pltpu.VMEM)] * n


def kernels_on_device(spans, planes, adjoint, checkpoints, checkpoint_step, metric,
                      helmholtz_inverse, wall_element, wall_local, wall_weight):
    _, zdev, q, _ = adjoint.shape
    wall_count = wall_element.shape[0]
    qp = -(-q // 16) * 16
    bulk, wide = q - 1, zdev * LANES
    half = bulk // 2
    shape = jax.ShapeDtypeStruct
    basis, diff, place = tables(spans, zdev, q, qp)
    basis, diff, place = jnp.asarray(basis), jnp.asarray(diff), jnp.asarray(place)
    operands = (checkpoint_step, adjoint.transpose(0, 2, 1, 3), checkpoints.transpose(0, 1, 3, 2, 4),
                helmholtz_inverse.transpose(1, 0, 2), metric, wall_element.T, wall_local.T,
                wall_weight, basis, diff, place)
    landing = [pltpu.SMEM(checkpoint_step.shape, jnp.int32)]
    landing += [pltpu.VMEM(a.shape, a.dtype) for a in operands[1:]]
    back, tback, weighted, squares = pl.pallas_call(
        functools.partial(step_kernel, spans, planes, zdev, q, qp),
        out_shape=(shape((3, spans, half, LANES), jnp.int16), shape((spans, 8, LANES), F32),
                   shape((zdev, wall_count // planes), F32),
                   shape((planes * spans, 1, LANES), F32)),
        in_specs=[pl.BlockSpec(memory_space=pl.ANY)] * len(operands),
        out_specs=tuple(vmem(4)),
        scratch_shapes=landing + [
            pltpu.VMEM((qp, 3 * wide), F32),
            pltpu.VMEM((2, qp, wide), F32),
            pltpu.VMEM((NSTEP, 2, q, zdev, LANES), F32),
            pltpu.VMEM((qp, 3 * wide), F32),
            pltpu.VMEM((NSTEP - 1, 2, qp, wide), F32),
            pltpu.VMEM((qp, wide), F32),
            pltpu.VMEM((qp, LANES), F32),
            pltpu.VMEM((zdev, qp, LANES), jnp.int16),
            pltpu.VMEM((zdev, spans, qp, LANES), jnp.int16),
            pltpu.VMEM((spans, 8, LANES), F32),
            pltpu.VMEM((3, spans, half, LANES), jnp.int16),
            pltpu.VMEM((spans, 8, LANES), F32),
            pltpu.VMEM((3, spans, half, LANES), jnp.int16),
            pltpu.VMEM((spans, 8, LANES), F32),
            pltpu.VMEM((NSTEP - 1, spans, bulk, LANES), BF16),
            pltpu.VMEM((NSTEP - 1, spans, bulk, LANES), BF16),
            pltpu.VMEM((spans, half, LANES), BF16),
            pltpu.VMEM((spans, half, LANES), BF16),
            pltpu.VMEM((3 * qp, wide), F32),
            pltpu.VMEM((3 * qp, wide), F32),
            pltpu.VMEM((qp, wide), F32),
            pltpu.VMEM((qp, wide), F32),
            pltpu.VMEM((zdev, spans * qp, 3 * LANES), BF16),
            pltpu.VMEM((3, spans, half, LANES), jnp.int16),
            pltpu.VMEM((spans, 8, LANES), F32),
            pltpu.VMEM((planes, 2, 2 * qp, 2 * LANES), BF16),
            pltpu.VMEM((planes, 2, LANES, 2 * LANES), F32),
            pltpu.VMEM((planes, spans, 8, LANES), F32),
            pltpu.VMEM((planes, spans, 8, LANES), F32),
            pltpu.VMEM((spans, 8, LANES), F32),
            pltpu.VMEM((spans, 8, LANES), F32),
            pltpu.VMEM((1, LANES), F32),
            pltpu.SemaphoreType.DMA((2, NKINDS + 2 * spans)),
            pltpu.SemaphoreType.DMA((len(operands),)),
            pltpu.SemaphoreType.DMA((4 + zdev + NSTEP,)),
        ],
        compiler_params=pltpu.CompilerParams(collective_id=0, has_side_effects=True),
        name="steps",
    )(*operands)
    field, gradient = pl.pallas_call(
        functools.partial(finish_kernel, spans, planes, zdev, q, float(spans * zdev * wall_count)),
        out_shape=(shape((3, q, zdev, LANES), F32), shape((zdev, wall_count // planes), F32)),
        in_specs=vmem(4),
        out_specs=tuple(vmem(2)),
        name="finish",
    )(back, tback, weighted, squares)
    return field.transpose(0, 2, 1, 3), gradient


def chosen(spans, planes, *args):
    zdev, q, elems = args[0].shape[1:]
    walls = args[5].shape[0]
    fits = (
        elems == LANES and spans == 2 * zdev and planes == zdev == 4
        and walls == planes * 2 * LANES and q % 16 == 1 and q < LANES
    )
    if fits:
        return kernels_on_device(spans, planes, *args)
    return on_device(*args)


def solution(mesh):
    placed = (
        P(None, "span", None, "plane"),
        P(None, None, "span", None, "plane"),
        P(),
        P(None, "plane"),
        P("span", None, None),
        P(),
        P(),
        P("span", None),
    )
    return jax.shard_map(
        functools.partial(chosen, mesh.shape["span"], mesh.shape["plane"]),
        mesh=mesh,
        in_specs=placed,
        out_specs=(P(None, "span", None, "plane"), P("span", "plane")),
        check_vma=False,
    )
```

```python
import functools

import jax
import jax.numpy as jnp
import ml_dtypes
import numpy as np
from jax import lax
from jax.experimental import pallas as pl
from jax.experimental.pallas import tpu as pltpu
from jax.sharding import PartitionSpec as P

P_SIZE = 8
NSTEP = 3


HIGHEST = lax.Precision.HIGHEST


def chebyshev_matrix(degree):
    points = np.arange(degree + 1)
    abscissa = np.cos(np.pi * points / degree)
    signed = np.where((points == 0) | (points == degree), 2.0, 1.0) * (-1.0) ** points
    spacing = abscissa[:, None] - abscissa[None, :] + np.eye(degree + 1)
    matrix = signed[:, None] / signed[None, :] / spacing
    return matrix - np.eye(degree + 1) * np.sum(matrix, axis=1)[:, None]


def fourier_table(length):
    row_index = np.arange(length)[:, None]
    column = np.arange(length)[None, :]
    wavenumber = (row_index + 1) // 2
    phase_angle = 2.0 * np.pi * wavenumber * column / length
    parity = row_index % 2
    base_rows = np.where(
        row_index == 0, 1.0, np.where(parity == 1, np.cos(phase_angle), np.sin(phase_angle))
    )
    row_scale = np.where(
        (row_index == 0) | (row_index == length - 1), 1.0 / np.sqrt(length), np.sqrt(2.0 / length)
    )
    return base_rows * row_scale


def transport(field_data, velocity, metric):
    side_nodes = P_SIZE + 1
    matrix = jnp.asarray(chebyshev_matrix(P_SIZE), jnp.float32)
    shaped = field_data.reshape(
        field_data.shape[0], field_data.shape[1], side_nodes, side_nodes, field_data.shape[3]
    )
    first_dir = jnp.einsum("ai,czibe->czabe", matrix, shaped, precision=HIGHEST).reshape(
        field_data.shape
    )
    second_dir = jnp.einsum("bi,czaie->czabe", matrix, shaped, precision=HIGHEST).reshape(
        field_data.shape
    )
    speed_data = velocity.astype(jnp.float32)
    return (
        field_data
        + speed_data[0] * (metric[0] * first_dir)
        + speed_data[1] * (metric[1] * second_dir)
    )


def forward_modes(gathered):
    basis_table = jnp.asarray(fourier_table(gathered.shape[1]), jnp.float32)
    return jnp.einsum("jz,czqe->cjqe", basis_table, gathered, precision=HIGHEST)


def backward_planes(solved):
    basis_table = jnp.asarray(fourier_table(solved.shape[1]), jnp.float32)
    return jnp.einsum("jz,cjqe->czqe", basis_table, solved, precision=HIGHEST)


def solve_modes(inverse_block, coefficients):
    return jnp.einsum("jqr,cjre->cjqe", inverse_block, coefficients, precision=HIGHEST)


def to_plane_layout(point_data):
    return lax.all_to_all(point_data, "span", split_axis=1, concat_axis=3, tiled=True)


def wall_terms(field_one, speed_one, flat_index, inside, wall_count):
    rows = field_one.shape[0]
    values = jnp.take(field_one.reshape(rows, -1), flat_index, axis=1)
    speeds = jnp.take(speed_one.reshape(rows, -1), flat_index, axis=1).astype(jnp.float32)
    product = jnp.where(inside, values * speeds, 0.0).reshape(rows, wall_count, 2)
    return jnp.sum(product, axis=2)


def on_device(
    adjoint,
    checkpoints,
    checkpoint_step,
    metric,
    helmholtz_inverse,
    wall_element,
    wall_local,
    wall_weight,
):
    planes_dev = adjoint.shape[1]
    elems_dev = adjoint.shape[3]
    wall_count = wall_element.shape[0]
    span_count = lax.axis_size("span")
    share = elems_dev // span_count
    all_modes = lax.all_gather(helmholtz_inverse, "span", axis=0, tiled=True)
    offset = lax.axis_index("plane") * elems_dev
    local_element = wall_element - offset
    inside = ((local_element >= 0) & (local_element < elems_dev)).reshape(-1)
    flat_index = (wall_local * elems_dev + jnp.clip(local_element, 0, elems_dev - 1)).reshape(-1)
    velocity = jnp.stack([
        lax.dynamic_index_in_dim(checkpoints, checkpoint_step[s], 0, keepdims=False)
        for s in range(NSTEP)
    ])
    velocity = lax.all_to_all(velocity, "span", split_axis=4, concat_axis=2, tiled=True)
    field = lax.all_to_all(adjoint, "span", split_axis=3, concat_axis=1, tiled=True)
    scale = lax.dynamic_slice_in_dim(metric, lax.axis_index("span") * share, share, 1)
    product = 0.0
    for substep in range(NSTEP):
        advected = transport(field, velocity[substep], scale)
        field = backward_planes(solve_modes(all_modes, forward_modes(advected)))
        product = product + field[1] * velocity[substep, 1].astype(jnp.float32)
    both = to_plane_layout(jnp.concatenate([field, product[None]], axis=0))
    gathered = jnp.take(both[3].reshape(planes_dev, -1), flat_index, axis=1)
    partial_sum = jnp.where(inside, gathered, 0.0).reshape(planes_dev, wall_count, 2).sum(axis=2)
    weighted = wall_weight * partial_sum
    grad_share = lax.psum_scatter(weighted, "plane", scatter_dimension=1, tiled=True)
    square_total = lax.psum(jnp.sum(grad_share * grad_share), ("span", "plane"))
    inverse_rms = lax.rsqrt(square_total / (planes_dev * span_count * wall_count) + 1e-06)
    return (both[:3], grad_share * inverse_rms)


MESH = pl.DeviceIdType.MESH
F32 = jnp.float32
BF16 = jnp.bfloat16
LANES = 128
NKINDS = 18
ORDER = (2, 6, 1, 7, 4, 3, 5)
MODE_ROWS = 64


def swap_blocks(parts, share):
    count = len(parts)
    width = count * share
    lane = lax.broadcasted_iota(jnp.int32, parts[0].shape, 1)
    k = count // 2
    while k:
        upper = (lane // (k * share)) % 2 == 1
        new = list(parts)
        for i in range(count):
            if (i // k) % 2 == 0:
                a, b = parts[i], parts[i + k]
                new[i] = jnp.where(upper, pltpu.roll(b, k * share, 1), a)
                new[i + k] = jnp.where(upper, b, pltpu.roll(a, width - k * share, 1))
        parts = new
        k //= 2
    return parts


def coded(x):
    top = jnp.maximum(jnp.max(jnp.abs(x), axis=0, keepdims=True), 1e-30)
    return jnp.round(x * (32767.0 / top)).astype(jnp.int32), top * (1.0 / 32767.0)


def remote(src, dst, sem_out, sem_in, target):
    return pltpu.make_async_remote_copy(
        src_ref=src, dst_ref=dst, send_sem=sem_out, recv_sem=sem_in,
        device_id=target, device_id_type=MESH,
    )


def mode_block(x, eye, q):
    diag = jnp.sum(jnp.where(eye, x, 0.0), axis=0, keepdims=True)
    off = jnp.where(eye, 0.0, x)
    row = lax.broadcasted_iota(jnp.int32, x.shape, 0)
    power = power_of(jnp.max(jnp.abs(off), axis=0, keepdims=True))
    power_d = power_of(jnp.abs(diag))
    unit = diag * (32767.0 * jnp.exp2(-power_d))
    high = jnp.round(unit)
    low = jnp.round((unit - high) * 32767.0)
    whole = jnp.round(off * (32767.0 * jnp.exp2(-power)))
    for i, extra in enumerate((power, power_d, high, low)):
        whole = jnp.where(row == q + i, extra, whole)
    lane = lax.broadcasted_iota(jnp.int32, (MODE_ROWS, LANES), 1)
    rest = whole[MODE_ROWS:MODE_ROWS + 24]
    aside = jnp.concatenate(
        [pltpu.roll(rest, q, 1), pltpu.roll(rest, 2 * q - LANES, 1), jnp.zeros((MODE_ROWS - 48, LANES), F32)], axis=0)
    return jnp.where(lane < q, whole[:MODE_ROWS], aside).astype(jnp.int32).astype(jnp.int16)


def power_of(top):
    return jnp.ceil(jnp.log2(jnp.maximum(top, 1e-30)))


def mode_matrix(block, eye, q):
    x = block.astype(jnp.int32).astype(F32)
    lane = lax.broadcasted_iota(jnp.int32, (24, LANES), 1)
    rest = jnp.where(lane < LANES - q, pltpu.roll(x[:24], LANES - q, 1), pltpu.roll(x[24:48], 2 * (LANES - q), 1))
    x = jnp.concatenate([x, rest, jnp.zeros((eye.shape[0] - MODE_ROWS - 24, LANES), F32)], axis=0)
    x = jnp.where(lax.broadcasted_iota(jnp.int32, x.shape, 1) < q, x, 0.0)
    scale = jnp.exp2(x[q:q + 1]) * (1.0 / 32767.0)
    diag = (x[q + 2:q + 3] + x[q + 3:q + 4] * (1.0 / 32767.0)) * (jnp.exp2(x[q + 1:q + 2]) * (1.0 / 32767.0))
    row = lax.broadcasted_iota(jnp.int32, x.shape, 0)
    return jnp.where(eye, diag, jnp.where(row < q, x, 0.0) * scale)


def step_kernel(spans, planes, zdev, q, qp,
                step_h, adj_h, ck_h, inv_h, metric_h, elem_h, local_h, weight_h, basis_h, diff_h, place_h, spread_h,
                back, tback, weighted_ref, srcv,
                step_ref, adj_ref, ck_ref, inv_ref, metric_ref, elem_ref, local_ref, weight_ref,
                basis_ref, diff_ref, place_ref, spread_ref,
                home, vhome, vf, xs_ref, vs_ref, v0_ref, padded, inv16, modes_ref, tail,
                snd, tsnd, rcv, trc, vsnd, vrcv, wsnd, wrc,
                coef, solved, product, kept, modes_cat, bsnd, tbsnd,
                picks, keeps, wall, rows_in, part, wrcv, square, sems, load_sem, local_sem):
    share = LANES // spans
    me, p = lax.axis_index("span"), lax.axis_index("plane")
    bulk = q - 1
    half = bulk // 2
    slabs = 3 * zdev
    wide = zdev * LANES

    barrier = pltpu.get_barrier_semaphore()
    for a in range(planes):
        for o in range(spans):
            if a or o:
                pl.semaphore_signal(
                    barrier, 1, device_id={"plane": (p + a) % planes, "span": (me + o) % spans},
                    device_id_type=MESH)
    names = ("inv", "step", "metric", "adj", "ck", "diff", "elem", "local", "place", "basis", "weight", "spread")
    pairs = ((inv_h, inv_ref), (step_h, step_ref), (metric_h, metric_ref), (adj_h, adj_ref), (ck_h, ck_ref),
             (diff_h, diff_ref), (elem_h, elem_ref), (local_h, local_ref), (place_h, place_ref),
             (basis_h, basis_ref), (weight_h, weight_ref), (spread_h, spread_ref))
    loads = {}
    for i, (src, dst) in enumerate(pairs):
        loads[names[i]] = pltpu.make_async_copy(src, dst, load_sem.at[i])
        loads[names[i]].start()

    def span_to(o):
        return {"span": (me + o) % spans}

    mate = me + 1 - 2 * (me % 2)
    to_mate = {"span": mate}
    most = slice(0, spans - 1)

    started = []

    def send(src, dst, kind, recv, target):
        remote(src, dst, sems.at[0, kind], sems.at[1, recv], target).start()

    def arrival(dst, recv):
        return remote(dst, dst, sems.at[0, 0], sems.at[1, recv], to_mate)

    def sent(kind, whole):
        started.append(remote(whole, whole, sems.at[0, kind], sems.at[1, 0], to_mate))

    def to_peers(kind, src, dst, whole):
        for o in range(1, spans):
            send(src((me + o) % spans), dst(me), kind, kind, span_to(o))
        sent(kind, whole)
        return arrival(whole, kind)

    padded[...] = jnp.zeros_like(padded)
    tail[...] = jnp.zeros_like(tail)
    home[bulk:, :] = jnp.zeros_like(home[bulk:, :])
    vhome[:, bulk:, :] = jnp.zeros_like(vhome[:, bulk:, :])
    xs_ref[bulk:, :] = jnp.zeros_like(xs_ref[bulk:, :])
    vs_ref[:, :, bulk:, :] = jnp.zeros_like(vs_ref[:, :, bulk:, :])
    v0_ref[bulk:, :] = jnp.zeros_like(v0_ref[bulk:, :])
    eye = (lax.broadcasted_iota(jnp.int32, (qp, LANES), 0)
           == lax.broadcasted_iota(jnp.int32, (qp, LANES), 1))

    loads["inv"].wait()
    for j in range(zdev):
        padded[:q, :q] = inv_ref[:, j, :]
        inv16[j] = mode_block(padded[...], eye, q)

    pl.semaphore_wait(barrier, spans * planes - 1)

    xpeer = {"plane": (p + 2) % planes}
    cpeer = {"plane": p + 1 - 2 * (p % 2)}
    px = (p + 2) % planes
    pc = p + 1 - 2 * (p % 2)
    pcx = (pc + 2) % planes
    single = NKINDS

    def block_of(i):
        return (me + spans - i) % spans

    for i in ORDER:
        send(inv16.at[p], modes_ref.at[p, me], 0, single + i, span_to(i))
    own = [pltpu.make_async_copy(inv16.at[j], modes_ref.at[j, me], local_sem.at[4 + j]) for j in range(zdev)]
    for c in own:
        c.start()
    for kind in range(4):
        sent(kind, modes_ref.at[0, most])

    def relay(i):
        s = block_of(i)
        block = modes_ref.at[p, s]
        arrival(block, single + i).wait_recv()
        send(block, block, 1, single + spans + i, xpeer)
        send(block, block, 2, 2, cpeer)

    def relay_across(i):
        block = modes_ref.at[px, block_of(i)]
        arrival(block, single + spans + i).wait_recv()
        send(block, block, 3, 3, cpeer)

    for name in ("step", "metric", "adj", "ck", "diff"):
        loads[name].wait()
    for t in range(NSTEP):
        slot = step_ref[t]
        for k in range(2):
            vf[t, k] = ck_ref[slot, k].astype(F32)
    for k in range(2):
        for z in range(zdev):
            vhome[k, :q, z * LANES:(z + 1) * LANES] = vf[0, k, :, z, :]
    for k in range(slabs):
        home[:q, k * LANES:(k + 1) * LANES] = adj_ref[k // zdev, :, k % zdev, :]
    here = metric_ref[...]
    first = jnp.concatenate([here[0:1]] * zdev, axis=1)
    second = jnp.concatenate([here[1:2]] * zdev, axis=1)
    v0 = vhome[0] * first
    v1 = vhome[1] * second
    scales = [None] * 3
    for c in (1, 0, 2):
        lanes = slice(c * wide, (c + 1) * wide)
        moved = transport_block(home[:, lanes], v0, v1, diff_ref, qp)
        home[:, lanes] = moved
        scales[c] = coded_component(moved, snd, c, spans, share, half)
    for k in range(slabs):
        tail[k % spans, k // spans:k // spans + 1, :] = home[bulk:q, k * LANES:(k + 1) * LANES]
    for k in range(2 * zdev):
        for t in range(1, NSTEP):
            tail[k, 1 + t:2 + t, :] = vf[t, k // zdev, bulk:q, k % zdev, :]
    for z in range(zdev):
        tail[z, 1 + NSTEP:2 + NSTEP, :] = vf[0, 1, bulk:q, z, :]
    parts = swap_blocks([tail[g] for g in range(spans)], share)
    for d in range(spans):
        tsnd[d] = jnp.concatenate([parts[d][:5]] + [scales[c][d] for c in range(3)], axis=0)

    fields = [None] * 3

    def send_field(c):
        fields[c] = to_peers(4 + c, lambda to: snd.at[c, to], lambda s: rcv.at[c, s], rcv.at[c, most])

    speeds = [None] * NSTEP

    def send_speed(t):
        parts = swap_blocks([vf[t, k // zdev, :bulk, k % zdev, :] for k in range(2 * zdev)], share)
        for d in range(spans):
            vsnd[t - 1, d] = parts[d].astype(BF16)
        speeds[t] = to_peers(7 + t, lambda to: vsnd.at[t - 1, to], lambda s: vrcv.at[t - 1, s], vrcv.at[t - 1, most])

    send_field(1)
    send_field(0)
    tails = to_peers(7, lambda to: tsnd.at[to], lambda s: trc.at[s], trc.at[most])
    for i in ORDER[:4]:
        relay(i)
    send_speed(1)
    for i in ORDER[4:]:
        relay(i)
    send_speed(2)
    for i in ORDER[:3]:
        relay_across(i)
    parts = []
    for g in range(spans):
        r = (g % 2) * half
        parts.append(vf[0, 1, r:r + half, g // 2, :])
    parts = swap_blocks(parts, share)
    for d in range(spans):
        wsnd[d] = parts[d].astype(BF16)
    speeds[0] = to_peers(10, lambda to: wsnd.at[to], lambda s: wrc.at[s], wrc.at[most])
    send_field(2)
    for c in range(3):
        own.append(pltpu.make_async_copy(snd.at[c, me], rcv.at[c, me], local_sem.at[c]))
    own.append(pltpu.make_async_copy(tsnd.at[me], trc.at[me], local_sem.at[3]))
    vown = [pltpu.make_async_copy(vsnd.at[t, me], vrcv.at[t, me], local_sem.at[4 + zdev + t]) for t in range(NSTEP - 1)]
    vown.append(pltpu.make_async_copy(wsnd.at[me], wrc.at[me], local_sem.at[3 + zdev + NSTEP]))
    for c in own[zdev:] + vown:
        c.start()
    for i in ORDER[3:5]:
        relay_across(i)

    lane = lax.broadcasted_iota(jnp.int32, (1, LANES), 1)
    rolled = pltpu.roll(metric_ref[...], (LANES - me * share) % LANES, 1)
    scale = jnp.where(lane < share, rolled, 0.0)
    k = share
    while k < LANES:
        scale = scale + pltpu.roll(scale, k, 1)
        k *= 2
    first = jnp.concatenate([scale[0:1]] * zdev, axis=1)
    second = jnp.concatenate([scale[1:2]] * zdev, axis=1)
    loads["elem"].wait()
    loads["local"].wait()
    pair = 2 * LANES
    base = p * LANES + me * share
    mode = lax.broadcasted_iota(jnp.int32, (qp, pair), 0)
    near = lax.broadcasted_iota(jnp.int32, (LANES, pair), 0) % share + base
    for piece in range(planes):
        lanes = slice(piece * pair, (piece + 1) * pair)
        for k in range(2):
            pick = jnp.where(local_ref[k:k + 1, lanes] == mode, 1.0, 0.0).astype(BF16)
            picks[piece, k] = jnp.concatenate([pick, pick], axis=0)
            keeps[piece, k] = jnp.where(elem_ref[k:k + 1, lanes] == near, 1.0, 0.0)
    for name in ("basis", "place", "weight", "spread"):
        loads[name].wait()

    for i in ORDER[5:]:
        relay_across(i)

    for c in own:
        c.wait()
    for c in (fields[1], fields[0], tails):
        c.wait_recv()

    def unpack(c):
        parts = [rcv[c, s].astype(jnp.int32).astype(F32) * trc[s, 5 + c:6 + c, :] for s in range(spans)]
        parts = swap_blocks(parts, share)
        for g in range(spans):
            k, r = c * zdev + g // 2, (g % 2) * half
            xs_ref[r:r + half, k * LANES:(k + 1) * LANES] = parts[g]

    parts = swap_blocks([trc[s] for s in range(spans)], share)
    for k in range(slabs):
        xs_ref[bulk:q, k * LANES:(k + 1) * LANES] = parts[k % spans][k // spans:k // spans + 1]
    for k in range(2 * zdev):
        z = k % zdev
        for t in range(1, NSTEP):
            vs_ref[t - 1, k // zdev, bulk:q, z * LANES:(z + 1) * LANES] = parts[k][1 + t:2 + t]
    for z in range(zdev):
        v0_ref[bulk:q, z * LANES:(z + 1) * LANES] = parts[z][1 + NSTEP:2 + NSTEP]
    unpack(0)
    unpack(1)

    for kind, plane in ((2, pc), (3, pcx)):
        arrival(modes_ref.at[plane, most], kind).wait_recv()
    for j in range(zdev):
        for s in range(spans):
            both = jnp.concatenate(split(mode_matrix(modes_ref[j, s], eye, q)), axis=1)
            modes_cat[j, s * qp:(s + 1) * qp, :] = dot(both, spread_ref[...]).astype(BF16)

    def step(group, t):
        count = len(group)
        rows = slice(group[0] * qp, (group[-1] + 1) * qp)
        if t:
            v0 = vs_ref[t - 1, 0] * first
            v1 = vs_ref[t - 1, 1] * second
        for c in group:
            x = xs_ref[:, c * wide:(c + 1) * wide]
            if t:
                x = transport_block(x, v0, v1, diff_ref, qp)
            coef[c * qp:(c + 1) * qp, :] = x
        coef[rows, :] = transform(coef[rows, :], basis_ref, False)
        block = lax.broadcasted_iota(jnp.int32, (1, count * LANES), 1) % LANES // share
        for j in range(zdev):
            lanes = slice(j * LANES, (j + 1) * LANES)
            x = jnp.concatenate([coef[c * qp:(c + 1) * qp, lanes] for c in group], axis=1)
            r = dot(modes_cat[j], stacked(x, bulk))
            acc = r[:qp]
            for s in range(1, spans):
                acc = jnp.where(block == s, r[s * qp:(s + 1) * qp], acc)
            for i, c in enumerate(group):
                solved[c * qp:(c + 1) * qp, lanes] = acc[:, i * LANES:(i + 1) * LANES]
        y = transform(solved[rows, :], basis_ref, True)
        for i, c in enumerate(group):
            xs_ref[:, c * wide:(c + 1) * wide] = y[i * qp:(i + 1) * qp]

    def unpack_speed(t):
        speeds[t].wait_recv()
        parts = swap_blocks([vrcv[t - 1, s].astype(F32) for s in range(spans)], share)
        for k in range(2 * zdev):
            z = k % zdev
            vs_ref[t - 1, k // zdev, :bulk, z * LANES:(z + 1) * LANES] = parts[k]

    one = slice(wide, 2 * wide)

    step((0, 1), 0)
    kept[...] = xs_ref[:, one]

    for c in vown:
        c.wait()
    unpack_speed(1)

    step((0, 1), 1)
    product[...] = xs_ref[:, one] * vs_ref[0, 1]

    unpack_speed(2)

    step((0, 1), 2)

    speeds[0].wait_recv()
    parts = swap_blocks([wrc[s].astype(F32) for s in range(spans)], share)
    for g in range(spans):
        z, r = g // 2, (g % 2) * half
        v0_ref[r:r + half, z * LANES:(z + 1) * LANES] = parts[g]
    product[...] += kept[...] * v0_ref[...] + xs_ref[:, one] * vs_ref[1, 1]

    high, low = split(product[...].T)
    left = jnp.concatenate([high, low], axis=1)
    for piece in range(planes):
        got = 0.0
        for k in range(2):
            keep = jnp.concatenate([keeps[piece, k]] * zdev, axis=0)
            got = got + dot(left, picks[piece, k]) * keep
        acc = dot(place_ref[...], jnp.concatenate(split(got), axis=0))
        acc = acc[:, :LANES] + pltpu.roll(acc[:, LANES:], zdev, 0)
        for s in range(spans):
            wall[piece, s] = acc[s * 8:(s + 1) * 8]
    for o in range(1, planes):
        to = (p + o) % planes
        send(wall.at[to], rows_in.at[p], 11, 11, {"plane": to})
    sent(11, wall.at[slice(0, planes - 1)])
    rown = pltpu.make_async_copy(wall.at[p], rows_in.at[p], local_sem.at[0])
    rown.start()

    scales = [None] * 3
    returned = []
    for c in (0, 1):
        scales[c] = coded_component(xs_ref[:, c * wide:(c + 1) * wide], bsnd, c, spans, share, half)
        returned.append(to_peers(13 + c, lambda to: bsnd.at[c, to], lambda s: back.at[c, s], back.at[c, most]))

    fields[2].wait_recv()
    unpack(2)

    step((2,), 0)

    rown.wait()
    arrival(rows_in.at[slice(0, planes - 1)], 11).wait_recv()
    part[...] = sum(rows_in[s] for s in range(planes))
    walls = to_peers(12, lambda to: part.at[to], lambda s: wrcv.at[s], wrcv.at[most])
    wown = pltpu.make_async_copy(part.at[me], wrcv.at[me], local_sem.at[4])
    wown.start()

    step((2,), 1)

    step((2,), 2)

    scales[2] = coded_component(xs_ref[:, 2 * wide:], bsnd, 2, spans, share, half)
    for k in range(slabs):
        tail[k % spans, k // spans:k // spans + 1, :] = xs_ref[bulk:q, k * LANES:(k + 1) * LANES]
    parts = swap_blocks([tail[g] for g in range(spans)], share)
    for d in range(spans):
        tbsnd[d] = jnp.concatenate([parts[d][:5]] + [scales[c][d] for c in range(3)], axis=0)
    returned.append(to_peers(15, lambda to: bsnd.at[2, to], lambda s: back.at[2, s], back.at[2, most]))
    returned.append(to_peers(16, lambda to: tbsnd.at[to], lambda s: tback.at[s], tback.at[most]))
    bown = [pltpu.make_async_copy(bsnd.at[c, me], back.at[c, me], local_sem.at[c]) for c in range(3)]
    bown.append(pltpu.make_async_copy(tbsnd.at[me], tback.at[me], local_sem.at[3]))
    for c in bown:
        c.start()

    wown.wait()
    walls.wait_recv()
    both = sum(wrcv[s] for s in range(spans))
    sums = jnp.concatenate([both[:zdev], both[zdev:]], axis=1)
    weight = weight_ref[:, pl.ds(pl.multiple_of(p * 2 * LANES, 2 * LANES), 2 * LANES)]
    weighted = weight * sums
    weighted_ref[...] = weighted
    sq = weighted * weighted
    square[...] = jnp.sum(sq[:, :LANES] + sq[:, LANES:], axis=0, keepdims=True)
    where = p * spans + me
    for a in range(planes):
        for o in range(spans):
            if a or o:
                send(square, srcv.at[where], 17, 17, {"plane": (p + a) % planes, "span": (me + o) % spans})
    others = srcv.at[slice(0, planes * spans - 1)]
    sent(17, others)
    srcv[where] = square[...]

    arrival(others, 17).wait_recv()
    for c in bown:
        c.wait()
    for c in returned:
        c.wait_recv()
    for c in started:
        c.wait_send()


def stacked(x, bulk):
    high, low = split(x)
    row = lax.broadcasted_iota(jnp.int32, (16, x.shape[1]), 0)
    last = x[bulk:bulk + 1]
    last_high = last.astype(BF16).astype(F32)
    ends = jnp.where(row == 1, last - last_high, jnp.where(row < 3, last_high, 0.0)).astype(BF16)
    return jnp.concatenate([high[:bulk], low[:bulk], high[:bulk], ends], axis=0)


def transport_block(x, v0, v1, diff_ref, qp):
    d = dot(diff_ref[...], stacked(x, qp - 16))
    return x + v0 * d[:qp] + v1 * d[qp:]


def coded_component(x, out, c, spans, share, half):
    parts = []
    for g in range(spans):
        z, r = g // 2, (g % 2) * half
        parts.append(x[r:r + half, z * LANES:(z + 1) * LANES])
    parts = swap_blocks(parts, share)
    scales = []
    for d in range(spans):
        whole, scale = coded(parts[d])
        out[c, d] = whole.astype(jnp.int16)
        scales.append(scale)
    return scales


def split(x):
    high = x.astype(BF16)
    return high, (x - high.astype(F32)).astype(BF16)


def dot(a, b, dims=((1,), (0,))):
    return lax.dot_general(a, b, (dims, ((), ())), preferred_element_type=F32)


def transform(x, basis_ref, back):
    high, low = split(x)
    left = jnp.concatenate([high, high, low], axis=1)
    parts = [basis_ref[0], basis_ref[1], basis_ref[0]]
    right = jnp.concatenate(parts, axis=1 if back else 0)
    return dot(left, right, ((1,), (1,)) if back else ((1,), (0,)))


def finish_kernel(spans, planes, zdev, q, count, back, tback, weighted_ref, srcv, out_ref, grad_ref):
    share = LANES // spans
    bulk = q - 1
    half = bulk // 2
    slabs = 3 * zdev
    squares = sum(srcv[n] for n in range(planes * spans))
    full = jnp.sum(squares, axis=1, keepdims=True)
    grad_ref[...] = weighted_ref[...] * lax.rsqrt(full / count + 1e-06)
    for c in range(3):
        parts = [back[c, s].astype(jnp.int32).astype(F32) * tback[s, 5 + c:6 + c, :] for s in range(spans)]
        parts = swap_blocks(parts, share)
        for g in range(spans):
            r = (g % 2) * half
            out_ref[c, r:r + half, g // 2, :] = parts[g]
    parts = swap_blocks([tback[s] for s in range(spans)], share)
    for k in range(slabs):
        out_ref[k // zdev, bulk:q, k % zdev, :] = parts[k % spans][k // spans:k // spans + 1]


def halves(table):
    high = table.astype(np.float32).astype(ml_dtypes.bfloat16)
    low = (table - high.astype(np.float64)).astype(np.float32).astype(ml_dtypes.bfloat16)
    return np.stack([high, low])


def tables(spans, zdev, q, qp):
    share = LANES // spans
    fourier = fourier_table(spans * zdev)
    order = np.array([s * zdev + z for z in range(zdev) for s in range(spans)])
    basis = np.kron(fourier[order][:, order].T, np.eye(share))
    side = P_SIZE + 1
    matrix = chebyshev_matrix(P_SIZE)
    diff = np.zeros((2 * qp, qp))
    diff[:q, :q] = np.kron(matrix, np.eye(side))
    diff[qp:qp + q, :q] = np.kron(np.eye(side), matrix)
    place = np.zeros((spans * 8, zdev * LANES), ml_dtypes.bfloat16)
    for s in range(spans):
        for z in range(zdev):
            at = z * LANES + s * share
            place[s * 8 + z, at:at + share] = 1.0
    bulk = q - 1
    spread = np.zeros((2 * LANES, 2 * LANES), ml_dtypes.bfloat16)
    for i in range(bulk):
        spread[i, i] = spread[i, bulk + i] = spread[LANES + i, 2 * bulk + i] = 1.0
    spread[bulk, 3 * bulk] = spread[bulk, 3 * bulk + 1] = spread[LANES + bulk, 3 * bulk + 2] = 1.0
    high, low = halves(diff)
    gap = np.zeros((2 * qp, LANES - qp), ml_dtypes.bfloat16)
    diff = np.concatenate([high, gap, low, gap], axis=1).astype(np.float32) @ spread.astype(np.float32)
    diff = diff.astype(ml_dtypes.bfloat16)
    place = np.concatenate([place, place], axis=1)
    return halves(basis), diff, place, spread


def vmem(n):
    return [pl.BlockSpec(memory_space=pltpu.VMEM)] * n


def kernels_on_device(spans, planes, adjoint, checkpoints, checkpoint_step, metric,
                      helmholtz_inverse, wall_element, wall_local, wall_weight):
    _, zdev, q, _ = adjoint.shape
    wall_count = wall_element.shape[0]
    qp = -(-q // 16) * 16
    bulk, wide = q - 1, zdev * LANES
    half = bulk // 2
    shape = jax.ShapeDtypeStruct
    constants = [jnp.asarray(a) for a in tables(spans, zdev, q, qp)]
    operands = (checkpoint_step, adjoint.transpose(0, 2, 1, 3), checkpoints.transpose(0, 1, 3, 2, 4),
                helmholtz_inverse.transpose(1, 0, 2), metric, wall_element.T, wall_local.T,
                wall_weight, *constants)
    landing = [pltpu.SMEM(checkpoint_step.shape, jnp.int32)]
    landing += [pltpu.VMEM(a.shape, a.dtype) for a in operands[1:]]
    back, tback, weighted, squares = pl.pallas_call(
        functools.partial(step_kernel, spans, planes, zdev, q, qp),
        out_shape=(shape((3, spans, half, LANES), jnp.int16), shape((spans, 8, LANES), F32),
                   shape((zdev, wall_count // planes), F32),
                   shape((planes * spans, 1, LANES), F32)),
        in_specs=[pl.BlockSpec(memory_space=pl.ANY)] * len(operands),
        out_specs=tuple(vmem(4)),
        scratch_shapes=landing + [
            pltpu.VMEM((qp, 3 * wide), F32),
            pltpu.VMEM((2, qp, wide), F32),
            pltpu.VMEM((NSTEP, 2, q, zdev, LANES), F32),
            pltpu.VMEM((qp, 3 * wide), F32),
            pltpu.VMEM((NSTEP - 1, 2, qp, wide), F32),
            pltpu.VMEM((qp, wide), F32),
            pltpu.VMEM((qp, LANES), F32),
            pltpu.VMEM((zdev, MODE_ROWS, LANES), jnp.int16),
            pltpu.VMEM((zdev, spans, MODE_ROWS, LANES), jnp.int16),
            pltpu.VMEM((spans, 8, LANES), F32),
            pltpu.VMEM((3, spans, half, LANES), jnp.int16),
            pltpu.VMEM((spans, 8, LANES), F32),
            pltpu.VMEM((3, spans, half, LANES), jnp.int16),
            pltpu.VMEM((spans, 8, LANES), F32),
            pltpu.VMEM((NSTEP - 1, spans, bulk, LANES), BF16),
            pltpu.VMEM((NSTEP - 1, spans, bulk, LANES), BF16),
            pltpu.VMEM((spans, half, LANES), BF16),
            pltpu.VMEM((spans, half, LANES), BF16),
            pltpu.VMEM((3 * qp, wide), F32),
            pltpu.VMEM((3 * qp, wide), F32),
            pltpu.VMEM((qp, wide), F32),
            pltpu.VMEM((qp, wide), F32),
            pltpu.VMEM((zdev, spans * qp, 2 * LANES), BF16),
            pltpu.VMEM((3, spans, half, LANES), jnp.int16),
            pltpu.VMEM((spans, 8, LANES), F32),
            pltpu.VMEM((planes, 2, 2 * qp, 2 * LANES), BF16),
            pltpu.VMEM((planes, 2, LANES, 2 * LANES), F32),
            pltpu.VMEM((planes, spans, 8, LANES), F32),
            pltpu.VMEM((planes, spans, 8, LANES), F32),
            pltpu.VMEM((spans, 8, LANES), F32),
            pltpu.VMEM((spans, 8, LANES), F32),
            pltpu.VMEM((1, LANES), F32),
            pltpu.SemaphoreType.DMA((2, NKINDS + 2 * spans)),
            pltpu.SemaphoreType.DMA((len(operands),)),
            pltpu.SemaphoreType.DMA((4 + zdev + NSTEP,)),
        ],
        compiler_params=pltpu.CompilerParams(collective_id=0, has_side_effects=True),
        name="steps",
    )(*operands)
    field, gradient = pl.pallas_call(
        functools.partial(finish_kernel, spans, planes, zdev, q, float(spans * zdev * wall_count)),
        out_shape=(shape((3, q, zdev, LANES), F32), shape((zdev, wall_count // planes), F32)),
        in_specs=vmem(4),
        out_specs=tuple(vmem(2)),
        name="finish",
    )(back, tback, weighted, squares)
    return field.transpose(0, 2, 1, 3), gradient


def chosen(spans, planes, *args):
    zdev, q, elems = args[0].shape[1:]
    walls = args[5].shape[0]
    fits = (
        elems == LANES and spans == 2 * zdev and planes == zdev == 4
        and walls == planes * 2 * LANES and q == (P_SIZE + 1) ** 2 and MODE_ROWS < q < 85
    )
    if fits:
        return kernels_on_device(spans, planes, *args)
    return on_device(*args)


def solution(mesh):
    placed = (
        P(None, "span", None, "plane"),
        P(None, None, "span", None, "plane"),
        P(),
        P(None, "plane"),
        P("span", None, None),
        P(),
        P(),
        P("span", None),
    )
    return jax.shard_map(
        functools.partial(chosen, mesh.shape["span"], mesh.shape["plane"]),
        mesh=mesh,
        in_specs=placed,
        out_specs=(P(None, "span", None, "plane"), P("span", "plane")),
        check_vma=False,
    )
```

```python
import functools

import jax
import jax.numpy as jnp
import ml_dtypes
import numpy as np
from jax import lax
from jax.experimental import pallas as pl
from jax.experimental.pallas import tpu as pltpu
from jax.sharding import PartitionSpec as P

P_SIZE = 8
NSTEP = 3


HIGHEST = lax.Precision.HIGHEST


def chebyshev_matrix(degree):
    points = np.arange(degree + 1)
    abscissa = np.cos(np.pi * points / degree)
    signed = np.where((points == 0) | (points == degree), 2.0, 1.0) * (-1.0) ** points
    spacing = abscissa[:, None] - abscissa[None, :] + np.eye(degree + 1)
    matrix = signed[:, None] / signed[None, :] / spacing
    return matrix - np.eye(degree + 1) * np.sum(matrix, axis=1)[:, None]


def fourier_table(length):
    row_index = np.arange(length)[:, None]
    column = np.arange(length)[None, :]
    wavenumber = (row_index + 1) // 2
    phase_angle = 2.0 * np.pi * wavenumber * column / length
    parity = row_index % 2
    base_rows = np.where(
        row_index == 0, 1.0, np.where(parity == 1, np.cos(phase_angle), np.sin(phase_angle))
    )
    row_scale = np.where(
        (row_index == 0) | (row_index == length - 1), 1.0 / np.sqrt(length), np.sqrt(2.0 / length)
    )
    return base_rows * row_scale


def transport(field_data, velocity, metric):
    side_nodes = P_SIZE + 1
    matrix = jnp.asarray(chebyshev_matrix(P_SIZE), jnp.float32)
    shaped = field_data.reshape(
        field_data.shape[0], field_data.shape[1], side_nodes, side_nodes, field_data.shape[3]
    )
    first_dir = jnp.einsum("ai,czibe->czabe", matrix, shaped, precision=HIGHEST).reshape(
        field_data.shape
    )
    second_dir = jnp.einsum("bi,czaie->czabe", matrix, shaped, precision=HIGHEST).reshape(
        field_data.shape
    )
    speed_data = velocity.astype(jnp.float32)
    return (
        field_data
        + speed_data[0] * (metric[0] * first_dir)
        + speed_data[1] * (metric[1] * second_dir)
    )


def forward_modes(gathered):
    basis_table = jnp.asarray(fourier_table(gathered.shape[1]), jnp.float32)
    return jnp.einsum("jz,czqe->cjqe", basis_table, gathered, precision=HIGHEST)


def backward_planes(solved):
    basis_table = jnp.asarray(fourier_table(solved.shape[1]), jnp.float32)
    return jnp.einsum("jz,cjqe->czqe", basis_table, solved, precision=HIGHEST)


def solve_modes(inverse_block, coefficients):
    return jnp.einsum("jqr,cjre->cjqe", inverse_block, coefficients, precision=HIGHEST)


def to_plane_layout(point_data):
    return lax.all_to_all(point_data, "span", split_axis=1, concat_axis=3, tiled=True)


def wall_terms(field_one, speed_one, flat_index, inside, wall_count):
    rows = field_one.shape[0]
    values = jnp.take(field_one.reshape(rows, -1), flat_index, axis=1)
    speeds = jnp.take(speed_one.reshape(rows, -1), flat_index, axis=1).astype(jnp.float32)
    product = jnp.where(inside, values * speeds, 0.0).reshape(rows, wall_count, 2)
    return jnp.sum(product, axis=2)


def on_device(
    adjoint,
    checkpoints,
    checkpoint_step,
    metric,
    helmholtz_inverse,
    wall_element,
    wall_local,
    wall_weight,
):
    planes_dev = adjoint.shape[1]
    elems_dev = adjoint.shape[3]
    wall_count = wall_element.shape[0]
    span_count = lax.axis_size("span")
    share = elems_dev // span_count
    all_modes = lax.all_gather(helmholtz_inverse, "span", axis=0, tiled=True)
    offset = lax.axis_index("plane") * elems_dev
    local_element = wall_element - offset
    inside = ((local_element >= 0) & (local_element < elems_dev)).reshape(-1)
    flat_index = (wall_local * elems_dev + jnp.clip(local_element, 0, elems_dev - 1)).reshape(-1)
    velocity = jnp.stack([
        lax.dynamic_index_in_dim(checkpoints, checkpoint_step[s], 0, keepdims=False)
        for s in range(NSTEP)
    ])
    velocity = lax.all_to_all(velocity, "span", split_axis=4, concat_axis=2, tiled=True)
    field = lax.all_to_all(adjoint, "span", split_axis=3, concat_axis=1, tiled=True)
    scale = lax.dynamic_slice_in_dim(metric, lax.axis_index("span") * share, share, 1)
    product = 0.0
    for substep in range(NSTEP):
        advected = transport(field, velocity[substep], scale)
        field = backward_planes(solve_modes(all_modes, forward_modes(advected)))
        product = product + field[1] * velocity[substep, 1].astype(jnp.float32)
    both = to_plane_layout(jnp.concatenate([field, product[None]], axis=0))
    gathered = jnp.take(both[3].reshape(planes_dev, -1), flat_index, axis=1)
    partial_sum = jnp.where(inside, gathered, 0.0).reshape(planes_dev, wall_count, 2).sum(axis=2)
    weighted = wall_weight * partial_sum
    grad_share = lax.psum_scatter(weighted, "plane", scatter_dimension=1, tiled=True)
    square_total = lax.psum(jnp.sum(grad_share * grad_share), ("span", "plane"))
    inverse_rms = lax.rsqrt(square_total / (planes_dev * span_count * wall_count) + 1e-06)
    return (both[:3], grad_share * inverse_rms)


MESH = pl.DeviceIdType.MESH
F32 = jnp.float32
BF16 = jnp.bfloat16
LANES = 128
NKINDS = 18
ORDER = (2, 6, 1, 7, 4, 3, 5)
MODE_ROWS = 64


def swap_blocks(parts, share):
    count = len(parts)
    width = count * share
    lane = lax.broadcasted_iota(jnp.int32, parts[0].shape, 1)
    k = count // 2
    while k:
        upper = (lane // (k * share)) % 2 == 1
        new = list(parts)
        for i in range(count):
            if (i // k) % 2 == 0:
                a, b = parts[i], parts[i + k]
                new[i] = jnp.where(upper, pltpu.roll(b, k * share, 1), a)
                new[i + k] = jnp.where(upper, b, pltpu.roll(a, width - k * share, 1))
        parts = new
        k //= 2
    return parts


def coded(x):
    top = jnp.maximum(jnp.max(jnp.abs(x), axis=0, keepdims=True), 1e-30)
    return jnp.round(x * (32767.0 / top)).astype(jnp.int32), top * (1.0 / 32767.0)


def remote(src, dst, sem_out, sem_in, target):
    return pltpu.make_async_remote_copy(
        src_ref=src, dst_ref=dst, send_sem=sem_out, recv_sem=sem_in,
        device_id=target, device_id_type=MESH,
    )


def mode_block(x, eye, q):
    diag = jnp.sum(jnp.where(eye, x, 0.0), axis=0, keepdims=True)
    off = jnp.where(eye, 0.0, x)
    row = lax.broadcasted_iota(jnp.int32, x.shape, 0)
    power = power_of(jnp.max(jnp.abs(off), axis=0, keepdims=True))
    power_d = power_of(jnp.abs(diag))
    unit = diag * (32767.0 * jnp.exp2(-power_d))
    high = jnp.round(unit)
    low = jnp.round((unit - high) * 32767.0)
    whole = jnp.round(off * (32767.0 * jnp.exp2(-power)))
    for i, extra in enumerate((power, power_d, high, low)):
        whole = jnp.where(row == q + i, extra, whole)
    lane = lax.broadcasted_iota(jnp.int32, (MODE_ROWS, LANES), 1)
    rest = whole[MODE_ROWS:MODE_ROWS + 24]
    aside = jnp.concatenate(
        [pltpu.roll(rest, q, 1), pltpu.roll(rest, 2 * q - LANES, 1), jnp.zeros((MODE_ROWS - 48, LANES), F32)], axis=0)
    return jnp.where(lane < q, whole[:MODE_ROWS], aside).astype(jnp.int32).astype(jnp.int16)


def power_of(top):
    return jnp.ceil(jnp.log2(jnp.maximum(top, 1e-30)))


def mode_matrix(block, eye, q):
    x = block.astype(jnp.int32).astype(F32)
    lane = lax.broadcasted_iota(jnp.int32, (24, LANES), 1)
    rest = jnp.where(lane < LANES - q, pltpu.roll(x[:24], LANES - q, 1), pltpu.roll(x[24:48], 2 * (LANES - q), 1))
    x = jnp.concatenate([x, rest, jnp.zeros((eye.shape[0] - MODE_ROWS - 24, LANES), F32)], axis=0)
    x = jnp.where(lax.broadcasted_iota(jnp.int32, x.shape, 1) < q, x, 0.0)
    scale = jnp.exp2(x[q:q + 1]) * (1.0 / 32767.0)
    diag = (x[q + 2:q + 3] + x[q + 3:q + 4] * (1.0 / 32767.0)) * (jnp.exp2(x[q + 1:q + 2]) * (1.0 / 32767.0))
    row = lax.broadcasted_iota(jnp.int32, x.shape, 0)
    return jnp.where(eye, diag, jnp.where(row < q, x, 0.0) * scale)


def step_kernel(spans, planes, zdev, q, qp,
                step_h, adj_h, ck_h, inv_h, metric_h, elem_h, local_h, weight_h, basis_h, diff_h, place_h, spread_h,
                back, tback, weighted_ref, srcv,
                step_ref, adj_ref, ck_ref, inv_ref, metric_ref, elem_ref, local_ref, weight_ref,
                basis_ref, diff_ref, place_ref, spread_ref,
                home, vhome, vf, xs_ref, vs_ref, v0_ref, padded, inv16, modes_ref, tail,
                snd, tsnd, rcv, trc, vsnd, vrcv, wsnd, wrc,
                coef, solved, product, kept, modes_cat, bsnd, tbsnd,
                picks, keeps, wall, rows_in, part, wrcv, square, sems, load_sem, local_sem):
    share = LANES // spans
    me, p = lax.axis_index("span"), lax.axis_index("plane")
    bulk = q - 1
    half = bulk // 2
    slabs = 3 * zdev
    wide = zdev * LANES

    barrier = pltpu.get_barrier_semaphore()
    for a in range(planes):
        for o in range(spans):
            if a or o:
                pl.semaphore_signal(
                    barrier, 1, device_id={"plane": (p + a) % planes, "span": (me + o) % spans},
                    device_id_type=MESH)
    names = ("inv", "step", "metric", "adj", "ck", "diff", "elem", "local", "place", "basis", "weight", "spread")
    pairs = ((inv_h, inv_ref), (step_h, step_ref), (metric_h, metric_ref), (adj_h, adj_ref), (ck_h, ck_ref),
             (diff_h, diff_ref), (elem_h, elem_ref), (local_h, local_ref), (place_h, place_ref),
             (basis_h, basis_ref), (weight_h, weight_ref), (spread_h, spread_ref))
    loads = {}
    for i, (src, dst) in enumerate(pairs):
        loads[names[i]] = pltpu.make_async_copy(src, dst, load_sem.at[i])
        loads[names[i]].start()

    def span_to(o):
        return {"span": (me + o) % spans}

    mate = me + 1 - 2 * (me % 2)
    to_mate = {"span": mate}
    most = slice(0, spans - 1)

    started = []

    def send(src, dst, kind, recv, target):
        remote(src, dst, sems.at[0, kind], sems.at[1, recv], target).start()

    def arrival(dst, recv):
        return remote(dst, dst, sems.at[0, 0], sems.at[1, recv], to_mate)

    def sent(kind, whole):
        started.append(remote(whole, whole, sems.at[0, kind], sems.at[1, 0], to_mate))

    def to_peers(kind, src, dst, whole):
        for o in range(1, spans):
            send(src((me + o) % spans), dst(me), kind, kind, span_to(o))
        sent(kind, whole)
        return arrival(whole, kind)

    padded[...] = jnp.zeros_like(padded)
    tail[...] = jnp.zeros_like(tail)
    home[bulk:, :] = jnp.zeros_like(home[bulk:, :])
    vhome[:, bulk:, :] = jnp.zeros_like(vhome[:, bulk:, :])
    xs_ref[bulk:, :] = jnp.zeros_like(xs_ref[bulk:, :])
    vs_ref[:, :, bulk:, :] = jnp.zeros_like(vs_ref[:, :, bulk:, :])
    v0_ref[bulk:, :] = jnp.zeros_like(v0_ref[bulk:, :])
    eye = (lax.broadcasted_iota(jnp.int32, (qp, LANES), 0)
           == lax.broadcasted_iota(jnp.int32, (qp, LANES), 1))

    loads["inv"].wait()
    for j in range(zdev):
        padded[:q, :q] = inv_ref[:, j, :]
        inv16[j] = mode_block(padded[...], eye, q)

    pl.semaphore_wait(barrier, spans * planes - 1)

    xpeer = {"plane": (p + 2) % planes}
    cpeer = {"plane": p + 1 - 2 * (p % 2)}
    px = (p + 2) % planes
    pc = p + 1 - 2 * (p % 2)
    pcx = (pc + 2) % planes
    single = NKINDS

    def block_of(i):
        return (me + spans - i) % spans

    for i in ORDER:
        send(inv16.at[p], modes_ref.at[p, me], 0, single + i, span_to(i))
    own = [pltpu.make_async_copy(inv16.at[j], modes_ref.at[j, me], local_sem.at[4 + j]) for j in range(zdev)]
    for c in own:
        c.start()
    for kind in range(4):
        sent(kind, modes_ref.at[0, most])

    def relay(i):
        s = block_of(i)
        block = modes_ref.at[p, s]
        arrival(block, single + i).wait_recv()
        send(block, block, 1, single + spans + i, xpeer)
        send(block, block, 2, 2, cpeer)

    def relay_across(i):
        block = modes_ref.at[px, block_of(i)]
        arrival(block, single + spans + i).wait_recv()
        send(block, block, 3, 3, cpeer)

    for name in ("step", "metric", "adj", "ck", "diff"):
        loads[name].wait()
    for t in range(NSTEP):
        slot = step_ref[t]
        for k in range(2):
            vf[t, k] = ck_ref[slot, k].astype(F32)
    for k in range(2):
        for z in range(zdev):
            vhome[k, :q, z * LANES:(z + 1) * LANES] = vf[0, k, :, z, :]
    for k in range(slabs):
        home[:q, k * LANES:(k + 1) * LANES] = adj_ref[k // zdev, :, k % zdev, :]
    here = metric_ref[...]
    first = jnp.concatenate([here[0:1]] * zdev, axis=1)
    second = jnp.concatenate([here[1:2]] * zdev, axis=1)
    v0 = vhome[0] * first
    v1 = vhome[1] * second
    scales = [None] * 3
    for c in (1, 0, 2):
        lanes = slice(c * wide, (c + 1) * wide)
        moved = transport_block(home[:, lanes], v0, v1, diff_ref, qp)
        home[:, lanes] = moved
        scales[c] = coded_component(moved, snd, c, spans, share, half)
    for k in range(slabs):
        tail[k % spans, k // spans:k // spans + 1, :] = home[bulk:q, k * LANES:(k + 1) * LANES]
    for k in range(2 * zdev):
        for t in range(1, NSTEP):
            tail[k, 1 + t:2 + t, :] = vf[t, k // zdev, bulk:q, k % zdev, :]
    for z in range(zdev):
        tail[z, 1 + NSTEP:2 + NSTEP, :] = vf[0, 1, bulk:q, z, :]
    parts = swap_blocks([tail[g] for g in range(spans)], share)
    for d in range(spans):
        tsnd[d] = jnp.concatenate([parts[d][:5]] + [scales[c][d] for c in range(3)], axis=0)

    fields = [None] * 3

    def send_field(c):
        fields[c] = to_peers(4 + c, lambda to: snd.at[c, to], lambda s: rcv.at[c, s], rcv.at[c, most])

    speeds = [None] * NSTEP

    def pack_speed(t):
        parts = swap_blocks([vf[t, k // zdev, :bulk, k % zdev, :] for k in range(2 * zdev)], share)
        for d in range(spans):
            vsnd[t - 1, d] = parts[d].astype(BF16)

    def send_speed(t):
        speeds[t] = to_peers(7 + t, lambda to: vsnd.at[t - 1, to], lambda s: vrcv.at[t - 1, s], vrcv.at[t - 1, most])

    send_field(1)
    send_field(0)
    tails = to_peers(7, lambda to: tsnd.at[to], lambda s: trc.at[s], trc.at[most])
    for i in ORDER[:4]:
        relay(i)
    pack_speed(1)
    send_speed(1)
    for i in ORDER[4:]:
        relay(i)
    pack_speed(2)
    for i in ORDER[:3]:
        relay_across(i)
    parts = []
    for g in range(spans):
        r = (g % 2) * half
        parts.append(vf[0, 1, r:r + half, g // 2, :])
    parts = swap_blocks(parts, share)
    for d in range(spans):
        wsnd[d] = parts[d].astype(BF16)
    for c in range(3):
        own.append(pltpu.make_async_copy(snd.at[c, me], rcv.at[c, me], local_sem.at[c]))
    own.append(pltpu.make_async_copy(tsnd.at[me], trc.at[me], local_sem.at[3]))
    vown = [pltpu.make_async_copy(vsnd.at[t, me], vrcv.at[t, me], local_sem.at[4 + zdev + t]) for t in range(NSTEP - 1)]
    vown.append(pltpu.make_async_copy(wsnd.at[me], wrc.at[me], local_sem.at[3 + zdev + NSTEP]))
    for c in own[zdev:] + vown:
        c.start()
    for i in ORDER[3:5]:
        relay_across(i)

    lane = lax.broadcasted_iota(jnp.int32, (1, LANES), 1)
    rolled = pltpu.roll(metric_ref[...], (LANES - me * share) % LANES, 1)
    scale = jnp.where(lane < share, rolled, 0.0)
    k = share
    while k < LANES:
        scale = scale + pltpu.roll(scale, k, 1)
        k *= 2
    first = jnp.concatenate([scale[0:1]] * zdev, axis=1)
    second = jnp.concatenate([scale[1:2]] * zdev, axis=1)
    loads["elem"].wait()
    loads["local"].wait()
    pair = 2 * LANES
    base = p * LANES + me * share
    mode = lax.broadcasted_iota(jnp.int32, (qp, pair), 0)
    near = lax.broadcasted_iota(jnp.int32, (LANES, pair), 0) % share + base
    for piece in range(planes):
        lanes = slice(piece * pair, (piece + 1) * pair)
        for k in range(2):
            pick = jnp.where(local_ref[k:k + 1, lanes] == mode, 1.0, 0.0).astype(BF16)
            picks[piece, k] = jnp.concatenate([pick, pick], axis=0)
            keeps[piece, k] = jnp.where(elem_ref[k:k + 1, lanes] == near, 1.0, 0.0)
    for name in ("basis", "place", "weight", "spread"):
        loads[name].wait()

    for i in ORDER[5:]:
        relay_across(i)

    for c in own:
        c.wait()
    for c in (fields[1], fields[0], tails):
        c.wait_recv()
    send_speed(2)

    def unpack(c):
        parts = [rcv[c, s].astype(jnp.int32).astype(F32) * trc[s, 5 + c:6 + c, :] for s in range(spans)]
        parts = swap_blocks(parts, share)
        for g in range(spans):
            k, r = c * zdev + g // 2, (g % 2) * half
            xs_ref[r:r + half, k * LANES:(k + 1) * LANES] = parts[g]

    parts = swap_blocks([trc[s] for s in range(spans)], share)
    for k in range(slabs):
        xs_ref[bulk:q, k * LANES:(k + 1) * LANES] = parts[k % spans][k // spans:k // spans + 1]
    for k in range(2 * zdev):
        z = k % zdev
        for t in range(1, NSTEP):
            vs_ref[t - 1, k // zdev, bulk:q, z * LANES:(z + 1) * LANES] = parts[k][1 + t:2 + t]
    for z in range(zdev):
        v0_ref[bulk:q, z * LANES:(z + 1) * LANES] = parts[z][1 + NSTEP:2 + NSTEP]
    unpack(0)
    unpack(1)

    for kind, plane in ((2, pc), (3, pcx)):
        arrival(modes_ref.at[plane, most], kind).wait_recv()
    for j in range(zdev):
        for s in range(spans):
            both = jnp.concatenate(split(mode_matrix(modes_ref[j, s], eye, q)), axis=1)
            modes_cat[j, s * qp:(s + 1) * qp, :] = dot(both, spread_ref[...]).astype(BF16)

    def step(group, t):
        count = len(group)
        rows = slice(group[0] * qp, (group[-1] + 1) * qp)
        if t:
            v0 = vs_ref[t - 1, 0] * first
            v1 = vs_ref[t - 1, 1] * second
        for c in group:
            x = xs_ref[:, c * wide:(c + 1) * wide]
            if t:
                x = transport_block(x, v0, v1, diff_ref, qp)
            coef[c * qp:(c + 1) * qp, :] = x
        coef[rows, :] = transform(coef[rows, :], basis_ref, False)
        block = lax.broadcasted_iota(jnp.int32, (1, count * LANES), 1) % LANES // share
        for j in range(zdev):
            lanes = slice(j * LANES, (j + 1) * LANES)
            x = jnp.concatenate([coef[c * qp:(c + 1) * qp, lanes] for c in group], axis=1)
            r = dot(modes_cat[j], stacked(x, bulk))
            acc = r[:qp]
            for s in range(1, spans):
                acc = jnp.where(block == s, r[s * qp:(s + 1) * qp], acc)
            for i, c in enumerate(group):
                solved[c * qp:(c + 1) * qp, lanes] = acc[:, i * LANES:(i + 1) * LANES]
        y = transform(solved[rows, :], basis_ref, True)
        for i, c in enumerate(group):
            xs_ref[:, c * wide:(c + 1) * wide] = y[i * qp:(i + 1) * qp]

    def unpack_speed(t):
        speeds[t].wait_recv()
        parts = swap_blocks([vrcv[t - 1, s].astype(F32) for s in range(spans)], share)
        for k in range(2 * zdev):
            z = k % zdev
            vs_ref[t - 1, k // zdev, :bulk, z * LANES:(z + 1) * LANES] = parts[k]

    one = slice(wide, 2 * wide)

    step((0, 1), 0)
    speeds[0] = to_peers(10, lambda to: wsnd.at[to], lambda s: wrc.at[s], wrc.at[most])
    send_field(2)
    kept[...] = xs_ref[:, one]

    for c in vown:
        c.wait()
    unpack_speed(1)

    step((0, 1), 1)
    product[...] = xs_ref[:, one] * vs_ref[0, 1]

    unpack_speed(2)

    step((0, 1), 2)

    speeds[0].wait_recv()
    parts = swap_blocks([wrc[s].astype(F32) for s in range(spans)], share)
    for g in range(spans):
        z, r = g // 2, (g % 2) * half
        v0_ref[r:r + half, z * LANES:(z + 1) * LANES] = parts[g]
    product[...] += kept[...] * v0_ref[...] + xs_ref[:, one] * vs_ref[1, 1]

    high, low = split(product[...].T)
    left = jnp.concatenate([high, low], axis=1)
    for piece in range(planes):
        got = 0.0
        for k in range(2):
            keep = jnp.concatenate([keeps[piece, k]] * zdev, axis=0)
            got = got + dot(left, picks[piece, k]) * keep
        acc = dot(place_ref[...], jnp.concatenate(split(got), axis=0))
        acc = acc[:, :LANES] + pltpu.roll(acc[:, LANES:], zdev, 0)
        for s in range(spans):
            wall[piece, s] = acc[s * 8:(s + 1) * 8]
    for o in range(1, planes):
        to = (p + o) % planes
        send(wall.at[to], rows_in.at[p], 11, 11, {"plane": to})
    sent(11, wall.at[slice(0, planes - 1)])
    rown = pltpu.make_async_copy(wall.at[p], rows_in.at[p], local_sem.at[0])
    rown.start()

    scales = [None] * 3
    returned = [None] * 3

    def give_back(c):
        returned[c] = to_peers(13 + c, lambda to: bsnd.at[c, to], lambda s: back.at[c, s], back.at[c, most])

    for c in (0, 1):
        scales[c] = coded_component(xs_ref[:, c * wide:(c + 1) * wide], bsnd, c, spans, share, half)
        if c == 0:
            give_back(c)

    fields[2].wait_recv()
    unpack(2)

    step((2,), 0)

    rown.wait()
    arrival(rows_in.at[slice(0, planes - 1)], 11).wait_recv()
    part[...] = sum(rows_in[s] for s in range(planes))
    walls = to_peers(12, lambda to: part.at[to], lambda s: wrcv.at[s], wrcv.at[most])
    wown = pltpu.make_async_copy(part.at[me], wrcv.at[me], local_sem.at[4])
    wown.start()
    give_back(1)

    step((2,), 1)

    step((2,), 2)

    scales[2] = coded_component(xs_ref[:, 2 * wide:], bsnd, 2, spans, share, half)
    for k in range(slabs):
        tail[k % spans, k // spans:k // spans + 1, :] = xs_ref[bulk:q, k * LANES:(k + 1) * LANES]
    parts = swap_blocks([tail[g] for g in range(spans)], share)
    for d in range(spans):
        tbsnd[d] = jnp.concatenate([parts[d][:5]] + [scales[c][d] for c in range(3)], axis=0)

    wown.wait()
    walls.wait_recv()
    both = sum(wrcv[s] for s in range(spans))
    sums = jnp.concatenate([both[:zdev], both[zdev:]], axis=1)
    weight = weight_ref[:, pl.ds(pl.multiple_of(p * 2 * LANES, 2 * LANES), 2 * LANES)]
    weighted = weight * sums
    weighted_ref[...] = weighted
    sq = weighted * weighted
    square[...] = jnp.sum(sq[:, :LANES] + sq[:, LANES:], axis=0, keepdims=True)
    where = p * spans + me
    for a in range(planes):
        for o in range(spans):
            if a or o:
                send(square, srcv.at[where], 17, 17, {"plane": (p + a) % planes, "span": (me + o) % spans})
    others = srcv.at[slice(0, planes * spans - 1)]
    sent(17, others)
    srcv[where] = square[...]

    tailed = to_peers(16, lambda to: tbsnd.at[to], lambda s: tback.at[s], tback.at[most])
    give_back(2)
    bown = [pltpu.make_async_copy(bsnd.at[c, me], back.at[c, me], local_sem.at[c]) for c in range(3)]
    bown.append(pltpu.make_async_copy(tbsnd.at[me], tback.at[me], local_sem.at[3]))
    for c in bown:
        c.start()

    arrival(others, 17).wait_recv()
    for c in bown:
        c.wait()
    for c in returned + [tailed]:
        c.wait_recv()
    for c in started:
        c.wait_send()


def stacked(x, bulk):
    high, low = split(x)
    row = lax.broadcasted_iota(jnp.int32, (16, x.shape[1]), 0)
    last = x[bulk:bulk + 1]
    last_high = last.astype(BF16).astype(F32)
    ends = jnp.where(row == 1, last - last_high, jnp.where(row < 3, last_high, 0.0)).astype(BF16)
    return jnp.concatenate([high[:bulk], low[:bulk], high[:bulk], ends], axis=0)


def transport_block(x, v0, v1, diff_ref, qp):
    d = dot(diff_ref[...], stacked(x, qp - 16))
    return x + v0 * d[:qp] + v1 * d[qp:]


def coded_component(x, out, c, spans, share, half):
    parts = []
    for g in range(spans):
        z, r = g // 2, (g % 2) * half
        parts.append(x[r:r + half, z * LANES:(z + 1) * LANES])
    parts = swap_blocks(parts, share)
    scales = []
    for d in range(spans):
        whole, scale = coded(parts[d])
        out[c, d] = whole.astype(jnp.int16)
        scales.append(scale)
    return scales


def split(x):
    high = x.astype(BF16)
    return high, (x - high.astype(F32)).astype(BF16)


def dot(a, b, dims=((1,), (0,))):
    return lax.dot_general(a, b, (dims, ((), ())), preferred_element_type=F32)


def transform(x, basis_ref, back):
    high, low = split(x)
    left = jnp.concatenate([high, high, low], axis=1)
    parts = [basis_ref[0], basis_ref[1], basis_ref[0]]
    right = jnp.concatenate(parts, axis=1 if back else 0)
    return dot(left, right, ((1,), (1,)) if back else ((1,), (0,)))


def finish_kernel(spans, planes, zdev, q, count, back, tback, weighted_ref, srcv, out_ref, grad_ref):
    share = LANES // spans
    bulk = q - 1
    half = bulk // 2
    slabs = 3 * zdev
    squares = sum(srcv[n] for n in range(planes * spans))
    full = jnp.sum(squares, axis=1, keepdims=True)
    grad_ref[...] = weighted_ref[...] * lax.rsqrt(full / count + 1e-06)
    for c in range(3):
        parts = [back[c, s].astype(jnp.int32).astype(F32) * tback[s, 5 + c:6 + c, :] for s in range(spans)]
        parts = swap_blocks(parts, share)
        for g in range(spans):
            r = (g % 2) * half
            out_ref[c, r:r + half, g // 2, :] = parts[g]
    parts = swap_blocks([tback[s] for s in range(spans)], share)
    for k in range(slabs):
        out_ref[k // zdev, bulk:q, k % zdev, :] = parts[k % spans][k // spans:k // spans + 1]


def halves(table):
    high = table.astype(np.float32).astype(ml_dtypes.bfloat16)
    low = (table - high.astype(np.float64)).astype(np.float32).astype(ml_dtypes.bfloat16)
    return np.stack([high, low])


def tables(spans, zdev, q, qp):
    share = LANES // spans
    fourier = fourier_table(spans * zdev)
    order = np.array([s * zdev + z for z in range(zdev) for s in range(spans)])
    basis = np.kron(fourier[order][:, order].T, np.eye(share))
    side = P_SIZE + 1
    matrix = chebyshev_matrix(P_SIZE)
    diff = np.zeros((2 * qp, qp))
    diff[:q, :q] = np.kron(matrix, np.eye(side))
    diff[qp:qp + q, :q] = np.kron(np.eye(side), matrix)
    place = np.zeros((spans * 8, zdev * LANES), ml_dtypes.bfloat16)
    for s in range(spans):
        for z in range(zdev):
            at = z * LANES + s * share
            place[s * 8 + z, at:at + share] = 1.0
    bulk = q - 1
    spread = np.zeros((2 * LANES, 2 * LANES), ml_dtypes.bfloat16)
    for i in range(bulk):
        spread[i, i] = spread[i, bulk + i] = spread[LANES + i, 2 * bulk + i] = 1.0
    spread[bulk, 3 * bulk] = spread[bulk, 3 * bulk + 1] = spread[LANES + bulk, 3 * bulk + 2] = 1.0
    high, low = halves(diff)
    gap = np.zeros((2 * qp, LANES - qp), ml_dtypes.bfloat16)
    diff = np.concatenate([high, gap, low, gap], axis=1).astype(np.float32) @ spread.astype(np.float32)
    diff = diff.astype(ml_dtypes.bfloat16)
    place = np.concatenate([place, place], axis=1)
    return halves(basis), diff, place, spread


def vmem(n):
    return [pl.BlockSpec(memory_space=pltpu.VMEM)] * n


def kernels_on_device(spans, planes, adjoint, checkpoints, checkpoint_step, metric,
                      helmholtz_inverse, wall_element, wall_local, wall_weight):
    _, zdev, q, _ = adjoint.shape
    wall_count = wall_element.shape[0]
    qp = -(-q // 16) * 16
    bulk, wide = q - 1, zdev * LANES
    half = bulk // 2
    shape = jax.ShapeDtypeStruct
    constants = [jnp.asarray(a) for a in tables(spans, zdev, q, qp)]
    operands = (checkpoint_step, adjoint.transpose(0, 2, 1, 3), checkpoints.transpose(0, 1, 3, 2, 4),
                helmholtz_inverse.transpose(1, 0, 2), metric, wall_element.T, wall_local.T,
                wall_weight, *constants)
    operands = tuple(pltpu.with_memory_space_constraint(a, pltpu.HBM) for a in operands)
    landing = [pltpu.SMEM(checkpoint_step.shape, jnp.int32)]
    landing += [pltpu.VMEM(a.shape, a.dtype) for a in operands[1:]]
    back, tback, weighted, squares = pl.pallas_call(
        functools.partial(step_kernel, spans, planes, zdev, q, qp),
        out_shape=(shape((3, spans, half, LANES), jnp.int16), shape((spans, 8, LANES), F32),
                   shape((zdev, wall_count // planes), F32),
                   shape((planes * spans, 1, LANES), F32)),
        in_specs=[pl.BlockSpec(memory_space=pltpu.HBM)] * len(operands),
        out_specs=tuple(vmem(4)),
        scratch_shapes=landing + [
            pltpu.VMEM((qp, 3 * wide), F32),
            pltpu.VMEM((2, qp, wide), F32),
            pltpu.VMEM((NSTEP, 2, q, zdev, LANES), F32),
            pltpu.VMEM((qp, 3 * wide), F32),
            pltpu.VMEM((NSTEP - 1, 2, qp, wide), F32),
            pltpu.VMEM((qp, wide), F32),
            pltpu.VMEM((qp, LANES), F32),
            pltpu.VMEM((zdev, MODE_ROWS, LANES), jnp.int16),
            pltpu.VMEM((zdev, spans, MODE_ROWS, LANES), jnp.int16),
            pltpu.VMEM((spans, 8, LANES), F32),
            pltpu.VMEM((3, spans, half, LANES), jnp.int16),
            pltpu.VMEM((spans, 8, LANES), F32),
            pltpu.VMEM((3, spans, half, LANES), jnp.int16),
            pltpu.VMEM((spans, 8, LANES), F32),
            pltpu.VMEM((NSTEP - 1, spans, bulk, LANES), BF16),
            pltpu.VMEM((NSTEP - 1, spans, bulk, LANES), BF16),
            pltpu.VMEM((spans, half, LANES), BF16),
            pltpu.VMEM((spans, half, LANES), BF16),
            pltpu.VMEM((3 * qp, wide), F32),
            pltpu.VMEM((3 * qp, wide), F32),
            pltpu.VMEM((qp, wide), F32),
            pltpu.VMEM((qp, wide), F32),
            pltpu.VMEM((zdev, spans * qp, 2 * LANES), BF16),
            pltpu.VMEM((3, spans, half, LANES), jnp.int16),
            pltpu.VMEM((spans, 8, LANES), F32),
            pltpu.VMEM((planes, 2, 2 * qp, 2 * LANES), BF16),
            pltpu.VMEM((planes, 2, LANES, 2 * LANES), F32),
            pltpu.VMEM((planes, spans, 8, LANES), F32),
            pltpu.VMEM((planes, spans, 8, LANES), F32),
            pltpu.VMEM((spans, 8, LANES), F32),
            pltpu.VMEM((spans, 8, LANES), F32),
            pltpu.VMEM((1, LANES), F32),
            pltpu.SemaphoreType.DMA((2, NKINDS + 2 * spans)),
            pltpu.SemaphoreType.DMA((len(operands),)),
            pltpu.SemaphoreType.DMA((4 + zdev + NSTEP,)),
        ],
        compiler_params=pltpu.CompilerParams(collective_id=0, has_side_effects=True, vmem_limit_bytes=24 << 20),
        name="steps",
    )(*operands)
    field, gradient = pl.pallas_call(
        functools.partial(finish_kernel, spans, planes, zdev, q, float(spans * zdev * wall_count)),
        out_shape=(shape((3, q, zdev, LANES), F32), shape((zdev, wall_count // planes), F32)),
        in_specs=vmem(4),
        out_specs=tuple(vmem(2)),
        compiler_params=pltpu.CompilerParams(vmem_limit_bytes=8 << 20),
        name="finish",
    )(back, tback, weighted, squares)
    return field.transpose(0, 2, 1, 3), gradient


def chosen(spans, planes, *args):
    zdev, q, elems = args[0].shape[1:]
    walls = args[5].shape[0]
    fits = (
        elems == LANES and spans == 2 * zdev and planes == zdev == 4
        and walls == planes * 2 * LANES and q == (P_SIZE + 1) ** 2 and MODE_ROWS < q < 85
    )
    if fits:
        return kernels_on_device(spans, planes, *args)
    return on_device(*args)


def solution(mesh):
    placed = (
        P(None, "span", None, "plane"),
        P(None, None, "span", None, "plane"),
        P(),
        P(None, "plane"),
        P("span", None, None),
        P(),
        P(),
        P("span", None),
    )
    return jax.shard_map(
        functools.partial(chosen, mesh.shape["span"], mesh.shape["plane"]),
        mesh=mesh,
        in_specs=placed,
        out_specs=(P(None, "span", None, "plane"), P("span", "plane")),
        check_vma=False,
    )
```
